32 devices in a mesh: seg: 8 (over y, x, core), dev: 4 (over z).
Axes of the slice: x: 2, y: 2, z: 4, core: 2. Of those that a mesh axis runs over, the one named last changes fastest.
Arguments:
- queries: bfloat16 [4096, 1536], P(('seg', 'dev')), may hold values from -12 to 12
- keys: bfloat16 [4096, 1536], P(('seg', 'dev')), may hold values from -12 to 12
- values: bfloat16 [4096, 1536], P(('seg', 'dev')), may hold values from -4 to 4
Outputs:
- grad_queries: bfloat16 [4096, 1536], P(('seg', 'dev'))
- grad_keys: bfloat16 [4096, 1536], P(('seg', 'dev'))
- grad_values: bfloat16 [4096, 1536], P(('seg', 'dev'))
The draws below stay inside these ranges and needn't reach their ends.
All inputs are finite; a program needn't handle non-finite values.
Results may differ from the reference program's by a relative error of at most 0.015.
Values may be sent and summed in bfloat16 or wider, within the bound.
No kernel may reach another device: no remote copies, remote signals or barrier semaphores. Data moves between devices by JAX's collectives and lax.ppermute only.
A program may use at most 128 MiB of HBM per device.

```python
import jax
import jax.numpy as jnp
from jax import lax

D = 1536
HEADS = 16
WINDOW = 256
FR_DEV = 128
SEG = 512
FRAMES = 4096
N_SEG = 8


def drawn_pair(key):
    query_base = jnp.clip(jax.random.normal(jax.random.fold_in(key, 11), (FRAMES, D), jnp.float32), -4.0, 4.0)
    key_base = jnp.clip(jax.random.normal(jax.random.fold_in(key, 12), (FRAMES, D), jnp.float32), -4.0, 4.0)
    return (query_base, key_base)


def draw_queries(key, part):
    return drawn_pair(key)[0].astype(jnp.bfloat16)


def draw_keys(key, part):
    return drawn_pair(key)[1].astype(jnp.bfloat16)


def levels(rng, shape, split, smallest, top_value):
    gain = 1.0
    for axis_at, shards_of in split:
        heights = jax.random.uniform(jax.random.fold_in(jax.random.fold_in(rng, 6), axis_at), (shards_of,), jnp.float32, smallest / len(split), top_value / len(split))
        gain = gain * jnp.repeat(jnp.exp(heights), shape[axis_at] // shards_of).reshape((-1,) + (1,) * (len(shape) - 1 - axis_at))
    return gain


def gaussian(own_key, dims, width, reach, cuts=(), kind=jnp.bfloat16):
    entries = width * jax.random.normal(own_key, dims, jnp.float32)
    if cuts:
        entries = entries * levels(own_key, dims, cuts, -0.22, 0.18)
    return jnp.clip(entries, -reach, reach).astype(kind)


def setup_inputs(seed: int = 0) -> dict:
    streams_of = jax.random.split(jax.random.key(seed), 4)
    queries = draw_queries(jax.random.fold_in(streams_of[3], 71), 0)
    keys = draw_keys(jax.random.fold_in(streams_of[3], 71), 0)
    values = gaussian(streams_of[2], (FRAMES, D), 1.0, 4.0, ((0, 32),))
    return {"queries": queries, "keys": keys, "values": values}


def student_pass(block_q, ext_keys, ext_values, target, first_row):
    row_count, model_width = block_q.shape
    ext_count = ext_keys.shape[0]
    reach_rows = ext_count - row_count
    head_dim = model_width // HEADS
    factor = head_dim ** -0.5
    query_heads = block_q.reshape(row_count, HEADS, head_dim).astype(jnp.float32)
    key_heads = ext_keys.reshape(ext_count, HEADS, head_dim).astype(jnp.float32)
    value_heads = ext_values.reshape(ext_count, HEADS, head_dim).astype(jnp.float32)
    scores = jnp.einsum("fhd,ehd->hfe", query_heads, key_heads) * factor
    query_pos = first_row + lax.iota(jnp.int32, row_count)
    key_pos = first_row - reach_rows + lax.iota(jnp.int32, ext_count)
    allowed = (key_pos[None, :] <= query_pos[:, None]) & (key_pos[None, :] >= query_pos[:, None] - reach_rows) & (key_pos[None, :] >= 0)
    scores = jnp.where(allowed[None], scores, -1e30)
    row_max = scores.max(-1, keepdims=True)
    numerators = jnp.exp(scores - row_max)
    probability = numerators / numerators.sum(-1, keepdims=True)
    weights = probability.astype(jnp.bfloat16).astype(jnp.float32)
    output = jnp.einsum("hfe,ehd->fhd", weights, value_heads).reshape(row_count, model_width)
    d_out = (128.0 * (output - target.astype(jnp.float32))).astype(jnp.bfloat16)
    d_out = d_out.astype(jnp.float32).reshape(row_count, HEADS, head_dim)
    grad_v = jnp.einsum("hfe,fhd->ehd", weights, d_out)
    d_prob = jnp.einsum("fhd,ehd->hfe", d_out, value_heads)
    row_inner = (probability * d_prob).sum(-1, keepdims=True)
    d_scores = (probability * (d_prob - row_inner) * factor).astype(jnp.bfloat16).astype(jnp.float32)
    grad_q = jnp.einsum("hfe,ehd->fhd", d_scores, key_heads)
    grad_k = jnp.einsum("hfe,fhd->ehd", d_scores, query_heads)
    return (grad_q.reshape(row_count, model_width), grad_k.reshape(ext_count, model_width), grad_v.reshape(ext_count, model_width))


def round_far(grad_rows):
    far_rows = lax.optimization_barrier(grad_rows[:WINDOW].astype(jnp.bfloat16)).astype(jnp.float32)
    return jnp.concatenate([far_rows, grad_rows[WINDOW:]], 0)


def teacher_block(query_block, seg_keys, seg_values):
    block_rows = query_block.shape[0]
    head_dim = D // HEADS
    factor = head_dim ** -0.5
    query_heads = query_block.reshape(block_rows, HEADS, head_dim).astype(jnp.float32)
    key_heads = seg_keys.reshape(-1, HEADS, head_dim).astype(jnp.float32)
    value_heads = seg_values.reshape(-1, HEADS, head_dim).astype(jnp.float32)
    scores = jnp.einsum("fhd,khd->hfk", query_heads, key_heads) * factor
    numerators = jnp.exp(scores - scores.max(-1, keepdims=True))
    totals = numerators.sum(-1, keepdims=True)
    weighted = jnp.einsum("hfk,khd->fhd", numerators.astype(jnp.bfloat16).astype(jnp.float32), value_heads)
    result = weighted / jnp.transpose(totals, (1, 0, 2))
    return result.reshape(block_rows, D).astype(jnp.bfloat16)


def teacher_segment(segment):
    seg_q, seg_k, seg_v = segment
    block_rows = 512 if SEG % 512 == 0 else SEG
    blocks = seg_q.reshape(SEG // block_rows, block_rows, D)
    outputs = lax.map(lambda query_block: teacher_block(query_block, seg_k, seg_v), blocks)
    return outputs.reshape(SEG, D)


def reference(queries, keys, values):
    target = lax.map(teacher_segment, (queries.reshape(N_SEG, SEG, D), keys.reshape(N_SEG, SEG, D), values.reshape(N_SEG, SEG, D)))
    target = target.reshape(FRAMES, D)
    zero_rows = jnp.zeros((WINDOW, D), keys.dtype)
    key_pad = jnp.concatenate([zero_rows, keys], 0)
    value_pad = jnp.concatenate([zero_rows, values], 0)
    ext_count = WINDOW + FR_DEV

    def advance(state_now, block_index):
        grad_k_pad, grad_v_pad = state_now
        first_row = (block_index * FR_DEV).astype(jnp.int32)
        block_q = lax.dynamic_slice_in_dim(queries, first_row, FR_DEV, 0)
        block_t = lax.dynamic_slice_in_dim(target, first_row, FR_DEV, 0)
        ext_keys = lax.dynamic_slice_in_dim(key_pad, first_row, ext_count, 0)
        ext_values = lax.dynamic_slice_in_dim(value_pad, first_row, ext_count, 0)
        grad_q, grad_k, grad_v = student_pass(block_q, ext_keys, ext_values, block_t, first_row)
        grad_k = round_far(grad_k)
        grad_v = round_far(grad_v)
        new_k = lax.dynamic_slice_in_dim(grad_k_pad, first_row, ext_count, 0) + grad_k
        new_v = lax.dynamic_slice_in_dim(grad_v_pad, first_row, ext_count, 0) + grad_v
        grad_k_pad = lax.dynamic_update_slice_in_dim(grad_k_pad, new_k, first_row, 0)
        grad_v_pad = lax.dynamic_update_slice_in_dim(grad_v_pad, new_v, first_row, 0)
        return (grad_k_pad, grad_v_pad), grad_q.astype(jnp.bfloat16)

    start_state = (jnp.zeros((WINDOW + FRAMES, D), jnp.float32), jnp.zeros((WINDOW + FRAMES, D), jnp.float32))
    final_state, grad_rows = lax.scan(advance, start_state, jnp.arange(FRAMES // FR_DEV, dtype=jnp.int32))
    grad_queries = grad_rows.reshape(FRAMES, D)
    grad_keys = final_state[0][WINDOW:].astype(jnp.bfloat16)
    grad_values = final_state[1][WINDOW:].astype(jnp.bfloat16)
    return (grad_queries, grad_keys, grad_values)
```

```python
import functools
import math

import jax
import jax.numpy as jnp
from jax import lax
from jax.experimental import pallas as pl
from jax.experimental.pallas import tpu as pltpu
from jax.sharding import PartitionSpec as P

HEADS = 16
WINDOW = 256
CHUNKS = 2
NEGATIVE = -1e30
LOG2E = math.log2(math.e)
BF16 = jnp.bfloat16
F32 = jnp.float32


SMEM_SPEC = pl.BlockSpec(memory_space=pltpu.SMEM)
VMEM_SPEC = pl.BlockSpec(memory_space=pltpu.VMEM)


def call(kernel, place, arrays, outs, scratch=(), flops=0):
    moved = sum(a.size * a.dtype.itemsize for a in arrays)
    moved += sum(math.prod(o.shape) * o.dtype.itemsize for o in outs)
    return pl.pallas_call(
        kernel,
        out_shape=tuple(outs),
        in_specs=[SMEM_SPEC] + [VMEM_SPEC] * len(arrays),
        out_specs=tuple([VMEM_SPEC] * len(outs)),
        scratch_shapes=list(scratch),
        cost_estimate=pl.CostEstimate(flops=flops, bytes_accessed=moved, transcendentals=0),
        compiler_params=pltpu.CompilerParams(vmem_limit_bytes=48 * 1024 * 1024),
    )(place, *arrays)


def shape(dims, dtype=BF16):
    return jax.ShapeDtypeStruct(dims, dtype)


class Plan:
    def __init__(self, rows, width, devs):
        self.rows, self.width, self.devs = rows, width, devs
        self.dim = width // HEADS
        self.local_heads = HEADS // devs
        self.local_width = width // devs
        self.chunks = CHUNKS if self.local_heads % CHUNKS == 0 else 1
        self.heads = self.local_heads // self.chunks
        self.chunk_width = self.heads * self.dim
        self.fold = 128 // math.gcd(self.chunk_width, 128)
        self.fold_rows = rows // self.fold
        self.piece = (self.fold_rows, self.fold * self.chunk_width)
        self.reach = WINDOW // rows
        self.seg_rows = rows * devs
        self.scale = self.dim ** (-0.5)


def folded(x, plan):
    parts = [x[i * plan.fold_rows : (i + 1) * plan.fold_rows] for i in range(plan.fold)]
    return parts[0] if plan.fold == 1 else jnp.concatenate(parts, axis=1)


def pack_kernel(plan, chunk, place, q_ref, k_ref, v_ref, *out_refs):
    me = place[1]
    for step, out_ref in enumerate(out_refs):
        start = pl.multiple_of((me ^ step) * plan.local_width, 128)
        for at, ref in enumerate((q_ref, k_ref, v_ref)):
            x = ref[:, pl.ds(start, plan.local_width)]
            x = x[:, chunk * plan.chunk_width : (chunk + 1) * plan.chunk_width]
            out_ref[at] = folded(x, plan)


def pack(plan, chunk, place, arrays):
    if plan.local_width % 128 == 0:
        outs = [shape((3,) + plan.piece) for _ in range(plan.devs)]
        return call(functools.partial(pack_kernel, plan, chunk), place, arrays, outs)
    pieces = []
    for step in range(plan.devs):
        start = (place[1] ^ step) * plan.local_width + chunk * plan.chunk_width
        taken = [lax.dynamic_slice_in_dim(a, start, plan.chunk_width, 1) for a in arrays]
        pieces.append(jnp.stack([folded(x, plan) for x in taken]))
    return pieces


def unpack_kernel(plan, place, *refs):
    me = place[1]
    piece_refs, out_refs = refs[:-3], refs[-3:]
    for step in range(plan.devs):
        start = pl.multiple_of((me ^ step) * plan.local_width, 128)
        for at, out_ref in enumerate(out_refs):
            rows = []
            for part in range(plan.fold):
                lanes = slice(part * plan.chunk_width, (part + 1) * plan.chunk_width)
                held = [
                    piece_refs[c * plan.devs + step][at, :, lanes] for c in range(plan.chunks)
                ]
                rows.append(held[0] if plan.chunks == 1 else jnp.concatenate(held, axis=1))
            out_ref[:, pl.ds(start, plan.local_width)] = (
                rows[0] if plan.fold == 1 else jnp.concatenate(rows, axis=0)
            )


def unpack(plan, place, pieces):
    if plan.local_width % 128 == 0:
        flat = [piece for chunk in pieces for piece in chunk]
        outs = [shape((plan.rows, plan.width)) for _ in range(3)]
        return call(functools.partial(unpack_kernel, plan), place, flat, outs)
    order = jnp.arange(plan.devs, dtype=jnp.int32) ^ place[1]
    chunks = []
    for chunk in pieces:
        x = jnp.take(jnp.stack(chunk), order, axis=0)
        x = x.reshape(plan.devs, 3, plan.fold_rows, plan.fold, plan.chunk_width)
        x = x.transpose(1, 3, 2, 0, 4)
        chunks.append(x.reshape(3, plan.rows, plan.devs, plan.chunk_width))
    out = jnp.concatenate(chunks, axis=3).reshape(3, plan.rows, plan.width)
    return out[0], out[1], out[2]


def exchange(plan, pieces):
    got = [pieces[0]] + [None] * (plan.devs - 1)
    for step in range(plan.devs - 1, 0, -1):
        pairs = [(i, i ^ step) for i in range(plan.devs)]
        got[step] = lax.ppermute(pieces[step], "dev", pairs)
    return got


def dot(a, b, over):
    return lax.dot_general(a, b, ((over[:1], over[1:]), ((), ())), preferred_element_type=F32)


def head_part(ref, index, head, part, plan):
    start = part * plan.chunk_width + head * plan.dim
    return ref[index + (slice(None), slice(start, start + plan.dim))]


def teacher_kernel(plan, place, *refs):
    me = place[1]
    piece_refs, (held_ref, target_ref) = refs[: plan.devs], refs[plan.devs :]
    for step, ref in enumerate(piece_refs):
        first = (me ^ step) * plan.rows
        for at in range(3):
            for head in range(plan.heads):
                for part in range(plan.fold):
                    start = pl.multiple_of(first + part * plan.fold_rows, plan.fold_rows)
                    held_ref[at, head, pl.ds(start, plan.fold_rows), :] = head_part(
                        ref, (at,), head, part, plan
                    )

    def body(i, _):
        head, block = i // plan.devs, i % plan.devs
        rows = pl.ds(pl.multiple_of(block * plan.rows, plan.rows), plan.rows)
        scores = dot(held_ref[0, head, rows, :], held_ref[1, head], (1, 1))
        top = scores.max(-1, keepdims=True)
        e = jnp.exp2((scores - top) * (plan.scale * LOG2E))
        total = e.sum(-1, keepdims=True)
        out = dot(e.astype(BF16), held_ref[2, head], (1, 0))
        target_ref[head, rows, :] = (out / total).astype(BF16)
        return 0

    lax.fori_loop(0, plan.heads * plan.devs, body, 0, unroll=4)


def teacher(plan, place, pieces):
    outs = [
        shape((3, plan.heads, plan.seg_rows, plan.dim)),
        shape((plan.heads, plan.seg_rows, plan.dim)),
    ]
    flops = 4 * plan.heads * plan.seg_rows * plan.seg_rows * plan.dim
    return call(functools.partial(teacher_kernel, plan), place, list(pieces), outs, flops=flops)


def student_block(plan, q, k, v, target, open_far):
    rows, reach = plan.rows, plan.reach
    scores = dot(q, k, (1, 1))
    query_at = lax.broadcasted_iota(jnp.int32, scores.shape, 0)
    key_at = lax.broadcasted_iota(jnp.int32, scores.shape, 1)
    allowed = (key_at >= query_at) & (key_at - reach * rows <= query_at)
    if open_far is not None:
        allowed &= key_at >= open_far
    scores = jnp.where(allowed, scores, NEGATIVE)
    top = scores.max(-1, keepdims=True)
    e = jnp.exp2((scores - top) * (plan.scale * LOG2E))
    probability = e * (1.0 / e.sum(-1, keepdims=True))
    weights = probability.astype(BF16)
    out = dot(weights, v, (1, 0))
    d_out = (128.0 * (out - target.astype(F32))).astype(BF16)
    d_prob = dot(d_out, v, (1, 1))
    inner = (probability * d_prob).sum(-1, keepdims=True)
    d_scores = (probability * (d_prob - inner) * plan.scale).astype(BF16)
    grad_q = dot(d_scores, k, (1, 0))
    grad_k = dot(d_scores, q, (0, 0))
    grad_v = dot(weights, d_out, (0, 0))
    return grad_q, grad_k, grad_v


def first_kernel(plan, place, held_ref, target_ref, halo_ref, gq_ref, gkv_ref, far_ref, ext, acc):
    seg = place[0]
    near = plan.reach * plan.rows
    for at in range(2):
        for head in range(plan.heads):
            for block in range(plan.reach):
                for part in range(plan.fold):
                    start = block * plan.rows + part * plan.fold_rows
                    ext[at, head, start : start + plan.fold_rows, :] = head_part(
                        halo_ref, (block, at), head, part, plan
                    )
            ext[at, head, near:, :] = held_ref[1 + at, head, :near, :]
    acc[...] = jnp.zeros_like(acc)

    def body(i, _):
        head, block = i // plan.reach, i % plan.reach
        start = pl.multiple_of(block * plan.rows, plan.rows)
        rows, keys = pl.ds(start, plan.rows), pl.ds(start, near + plan.rows)
        open_far = jnp.where(seg == 0, near - start, 0)
        gq, gk, gv = student_block(
            plan,
            held_ref[0, head, rows, :],
            ext[0, head, keys, :],
            ext[1, head, keys, :],
            target_ref[head, rows, :],
            open_far,
        )
        gq_ref[head, rows, :] = gq.astype(BF16)
        acc[0, head, keys, :] += gk
        acc[1, head, keys, :] += gv
        return 0

    lax.fori_loop(0, plan.heads * plan.reach, body, 0, unroll=2)
    gkv_ref[...] = acc[:, :, near:, :]
    for at in range(2):
        for block in range(plan.reach):
            for part in range(plan.fold):
                start = block * plan.rows + part * plan.fold_rows
                for head in range(plan.heads):
                    lane = part * plan.chunk_width + head * plan.dim
                    far_ref[block, at, :, lane : lane + plan.dim] = acc[
                        at, head, start : start + plan.fold_rows, :
                    ].astype(BF16)


def first_blocks(plan, place, held, target, halo):
    near = plan.reach * plan.rows
    outs = [
        shape((plan.heads, near, plan.dim)),
        shape((2, plan.heads, near, plan.dim), F32),
        shape((plan.reach, 2) + plan.piece),
    ]
    scratch = [
        pltpu.VMEM((2, plan.heads, 2 * near, plan.dim), BF16),
        pltpu.VMEM((2, plan.heads, 2 * near, plan.dim), F32),
    ]
    flops = 12 * plan.heads * near * (near + plan.rows) * plan.dim
    return call(
        functools.partial(first_kernel, plan), place, [held, target, halo], outs, scratch, flops
    )


def rest_kernel(plan, place, held_ref, target_ref, start_ref, gq_ref, acc):
    near = plan.reach * plan.rows
    acc[:, :, :near, :] = start_ref[...]
    acc[:, :, near:, :] = jnp.zeros((2, plan.heads, plan.seg_rows - near, plan.dim), F32)
    count = plan.devs - plan.reach

    def body(i, _):
        head, block = i // count, i % count
        start = pl.multiple_of(block * plan.rows, plan.rows)
        rows = pl.ds(pl.multiple_of(start + near, plan.rows), plan.rows)
        keys = pl.ds(start, near + plan.rows)
        gq, gk, gv = student_block(
            plan,
            held_ref[0, head, rows, :],
            held_ref[1, head, keys, :],
            held_ref[2, head, keys, :],
            target_ref[head, rows, :],
            None,
        )
        gq_ref[head, pl.ds(start, plan.rows), :] = gq.astype(BF16)
        acc[0, head, keys, :] += gk
        acc[1, head, keys, :] += gv
        return 0

    lax.fori_loop(0, plan.heads * count, body, 0, unroll=2)


def rest_blocks(plan, place, held, target, start):
    near = plan.reach * plan.rows
    outs = [
        shape((plan.heads, plan.seg_rows - near, plan.dim)),
        shape((2, plan.heads, plan.seg_rows, plan.dim), F32),
    ]
    flops = 12 * plan.heads * (plan.seg_rows - near) * (near + plan.rows) * plan.dim
    return call(
        functools.partial(rest_kernel, plan), place, [held, target, start], outs, (), flops
    )


def finish_kernel(plan, place, gq_first, gq_rest, gkv, far, *refs):
    me = place[1]
    out_refs, (grads,) = refs[: plan.devs], refs[plan.devs :]
    near = plan.reach * plan.rows
    last = plan.seg_rows - near
    for head in range(plan.heads):
        grads[0, head, :near, :] = gq_first[head]
        grads[0, head, near:, :] = gq_rest[head]
        for at in range(2):
            grads[1 + at, head, :last, :] = gkv[at, head, :last, :].astype(BF16)
            for block in range(plan.reach):
                for part in range(plan.fold):
                    start = last + block * plan.rows + part * plan.fold_rows
                    span = slice(start, start + plan.fold_rows)
                    back = head_part(far, (block, at), head, part, plan).astype(F32)
                    grads[1 + at, head, span, :] = (gkv[at, head, span, :] + back).astype(BF16)
    for step, out_ref in enumerate(out_refs):
        first = (me ^ step) * plan.rows
        for at in range(3):
            for part in range(plan.fold):
                start = pl.multiple_of(first + part * plan.fold_rows, plan.fold_rows)
                held = [
                    grads[at, head, pl.ds(start, plan.fold_rows), :] for head in range(plan.heads)
                ]
                lane = part * plan.chunk_width
                out_ref[at, :, lane : lane + plan.chunk_width] = (
                    held[0] if plan.heads == 1 else jnp.concatenate(held, axis=1)
                )


def finish(plan, place, gq_first, gq_rest, gkv, far):
    outs = [shape((3,) + plan.piece) for _ in range(plan.devs)]
    scratch = [pltpu.VMEM((3, plan.heads, plan.seg_rows, plan.dim), BF16)]
    arrays = [gq_first, gq_rest, gkv, far]
    return call(functools.partial(finish_kernel, plan), place, arrays, outs, scratch)


def local(queries, keys, values):
    rows, width = queries.shape
    plan = Plan(rows, width, lax.axis_size("dev"))
    seg_count = lax.axis_size("seg")
    onward = [(i, i + 1) for i in range(seg_count - 1)]
    backward = [(i + 1, i) for i in range(seg_count - 1)]
    me = lax.axis_index("dev")
    place = jnp.stack([lax.axis_index("seg"), me]).astype(jnp.int32)
    arrays = [queries, keys, values]
    arrived = [exchange(plan, pack(plan, c, place, arrays)) for c in range(plan.chunks)]
    returned = []
    for pieces in arrived:
        halo = jnp.stack(
            [
                lax.select_n((plan.devs - plan.reach + b) ^ me, *[p[1:] for p in pieces])
                for b in range(plan.reach)
            ]
        )
        halo = lax.ppermute(halo, "seg", onward)
        held, target = teacher(plan, place, pieces)
        gq_first, gkv, far = first_blocks(plan, place, held, target, halo)
        far = lax.ppermute(far, "seg", backward)
        gq_rest, gkv = rest_blocks(plan, place, held, target, gkv)
        returned.append(exchange(plan, finish(plan, place, gq_first, gq_rest, gkv, far)))
    return tuple(unpack(plan, place, returned))


def solution(mesh):
    spec = P(("seg", "dev"), None)
    return jax.shard_map(
        local, mesh=mesh, in_specs=(spec,) * 3, out_specs=(spec,) * 3, check_vma=False
    )
```

```python
import functools
import math

import jax
import jax.numpy as jnp
from jax import lax
from jax.experimental import pallas as pl
from jax.experimental.pallas import tpu as pltpu
from jax.sharding import PartitionSpec as P


HEADS = 16
WINDOW = 256
CHUNKS = 2
NEGATIVE = -1e30
LOG2E = math.log2(math.e)
BF16 = jnp.bfloat16
F32 = jnp.float32


SMEM_SPEC = pl.BlockSpec(memory_space=pltpu.SMEM)
VMEM_SPEC = pl.BlockSpec(memory_space=pltpu.VMEM)
HBM_SPEC = pl.BlockSpec(memory_space=pltpu.HBM)


def call(kernel, place, arrays, outs, scratch=(), flops=0, spec=VMEM_SPEC):
    moved = sum(a.size * a.dtype.itemsize for a in arrays)
    moved += sum(math.prod(o.shape) * o.dtype.itemsize for o in outs)
    return pl.pallas_call(
        kernel,
        out_shape=tuple(outs),
        in_specs=[SMEM_SPEC] + [spec] * len(arrays),
        out_specs=tuple([VMEM_SPEC] * len(outs)),
        scratch_shapes=list(scratch),
        cost_estimate=pl.CostEstimate(flops=flops, bytes_accessed=moved, transcendentals=0),
        compiler_params=pltpu.CompilerParams(vmem_limit_bytes=48 * 1024 * 1024),
    )(place, *arrays)


def shape(dims, dtype=BF16):
    return jax.ShapeDtypeStruct(dims, dtype)


class Plan:
    def __init__(self, rows, width, devs):
        self.rows, self.width, self.devs = rows, width, devs
        self.dim = width // HEADS
        self.local_heads = HEADS // devs
        self.local_width = width // devs
        self.chunks = CHUNKS if self.local_heads % CHUNKS == 0 else 1
        self.heads = self.local_heads // self.chunks
        self.chunk_width = self.heads * self.dim
        self.fold = 128 // math.gcd(self.chunk_width, 128)
        self.fold_rows = rows // self.fold
        self.piece = (self.fold_rows, self.fold * self.chunk_width)
        self.reach = WINDOW // rows
        self.seg_rows = rows * devs
        self.scale = self.dim ** (-0.5)


def folded(x, plan):
    parts = [x[i * plan.fold_rows : (i + 1) * plan.fold_rows] for i in range(plan.fold)]
    return parts[0] if plan.fold == 1 else jnp.concatenate(parts, axis=1)


def pack_kernel(plan, chunk, place, *refs):
    me = place[1]
    in_refs, out_refs = refs[:3], refs[3 : 3 + plan.devs]
    held, sems = refs[3 + plan.devs :]
    copies = [pltpu.make_async_copy(r, held.at[i], sems.at[i]) for i, r in enumerate(in_refs)]
    for copy in copies:
        copy.start()
    for at, copy in enumerate(copies):
        copy.wait()
        for step, out_ref in enumerate(out_refs):
            start = pl.multiple_of((me ^ step) * plan.local_width, 128)
            x = held[at, :, pl.ds(start, plan.local_width)]
            x = x[:, chunk * plan.chunk_width : (chunk + 1) * plan.chunk_width]
            out_ref[at] = folded(x, plan)


def pack(plan, chunk, place, arrays):
    if plan.local_width % 128 == 0:
        outs = [shape((3,) + plan.piece) for _ in range(plan.devs)]
        scratch = [
            pltpu.VMEM((3, plan.rows, plan.width), BF16),
            pltpu.SemaphoreType.DMA((3,)),
        ]
        kernel = functools.partial(pack_kernel, plan, chunk)
        return call(kernel, place, arrays, outs, scratch, spec=HBM_SPEC)
    pieces = []
    for step in range(plan.devs):
        start = (place[1] ^ step) * plan.local_width + chunk * plan.chunk_width
        taken = [lax.dynamic_slice_in_dim(a, start, plan.chunk_width, 1) for a in arrays]
        pieces.append(jnp.stack([folded(x, plan) for x in taken]))
    return pieces


def unpack_kernel(plan, place, *refs):
    me = place[1]
    piece_refs, out_refs = refs[:-3], refs[-3:]
    for step in range(plan.devs):
        start = pl.multiple_of((me ^ step) * plan.local_width, 128)
        for at, out_ref in enumerate(out_refs):
            rows = []
            for part in range(plan.fold):
                lanes = slice(part * plan.chunk_width, (part + 1) * plan.chunk_width)
                held = [
                    piece_refs[c * plan.devs + step][at, :, lanes] for c in range(plan.chunks)
                ]
                rows.append(held[0] if plan.chunks == 1 else jnp.concatenate(held, axis=1))
            out_ref[:, pl.ds(start, plan.local_width)] = (
                rows[0] if plan.fold == 1 else jnp.concatenate(rows, axis=0)
            )


def unpack(plan, place, pieces):
    if plan.local_width % 128 == 0:
        flat = [piece for chunk in pieces for piece in chunk]
        outs = [shape((plan.rows, plan.width)) for _ in range(3)]
        return call(functools.partial(unpack_kernel, plan), place, flat, outs)
    order = jnp.arange(plan.devs, dtype=jnp.int32) ^ place[1]
    chunks = []
    for chunk in pieces:
        x = jnp.take(jnp.stack(chunk), order, axis=0)
        x = x.reshape(plan.devs, 3, plan.fold_rows, plan.fold, plan.chunk_width)
        x = x.transpose(1, 3, 2, 0, 4)
        chunks.append(x.reshape(3, plan.rows, plan.devs, plan.chunk_width))
    out = jnp.concatenate(chunks, axis=3).reshape(3, plan.rows, plan.width)
    return out[0], out[1], out[2]


def exchange(plan, pieces):
    got = [pieces[0]] + [None] * (plan.devs - 1)
    for step in range(plan.devs - 1, 0, -1):
        pairs = [(i, i ^ step) for i in range(plan.devs)]
        got[step] = lax.ppermute(pieces[step], "dev", pairs)
    return got


def dot(a, b, over):
    return lax.dot_general(a, b, ((over[:1], over[1:]), ((), ())), preferred_element_type=F32)


def head_part(ref, index, head, part, plan):
    start = part * plan.chunk_width + head * plan.dim
    return ref[index + (slice(None), slice(start, start + plan.dim))]


def teacher_kernel(plan, place, *refs):
    me = place[1]
    piece_refs, (held_ref, target_ref) = refs[: plan.devs], refs[plan.devs :]
    for step, ref in enumerate(piece_refs):
        first = (me ^ step) * plan.rows
        for at in range(3):
            for head in range(plan.heads):
                for part in range(plan.fold):
                    start = pl.multiple_of(first + part * plan.fold_rows, plan.fold_rows)
                    held_ref[at, head, pl.ds(start, plan.fold_rows), :] = head_part(
                        ref, (at,), head, part, plan
                    )

    def body(i, _):
        head, block = i // plan.devs, i % plan.devs
        rows = pl.ds(pl.multiple_of(block * plan.rows, plan.rows), plan.rows)
        scores = dot(held_ref[0, head, rows, :], held_ref[1, head], (1, 1))
        top = scores.max(-1, keepdims=True)
        e = jnp.exp2((scores - top) * (plan.scale * LOG2E))
        total = e.sum(-1, keepdims=True)
        out = dot(e.astype(BF16), held_ref[2, head], (1, 0))
        target_ref[head, rows, :] = (out / total).astype(BF16)
        return 0

    lax.fori_loop(0, plan.heads * plan.devs, body, 0, unroll=4)


def teacher(plan, place, pieces):
    outs = [
        shape((3, plan.heads, plan.seg_rows, plan.dim)),
        shape((plan.heads, plan.seg_rows, plan.dim)),
    ]
    flops = 4 * plan.heads * plan.seg_rows * plan.seg_rows * plan.dim
    return call(functools.partial(teacher_kernel, plan), place, list(pieces), outs, flops=flops)


def student_block(plan, q, k, v, target, open_far):
    rows, reach = plan.rows, plan.reach
    scores = dot(q, k, (1, 1))
    query_at = lax.broadcasted_iota(jnp.int32, scores.shape, 0)
    key_at = lax.broadcasted_iota(jnp.int32, scores.shape, 1)
    allowed = (key_at >= query_at) & (key_at - reach * rows <= query_at)
    if open_far is not None:
        allowed &= key_at >= open_far
    scores = jnp.where(allowed, scores, NEGATIVE)
    top = scores.max(-1, keepdims=True)
    e = jnp.exp2((scores - top) * (plan.scale * LOG2E))
    probability = e * (1.0 / e.sum(-1, keepdims=True))
    weights = probability.astype(BF16)
    out = dot(weights, v, (1, 0))
    d_out = (128.0 * (out - target.astype(F32))).astype(BF16)
    d_prob = dot(d_out, v, (1, 1))
    inner = (probability * d_prob).sum(-1, keepdims=True)
    d_scores = (probability * (d_prob - inner) * plan.scale).astype(BF16)
    grad_q = dot(d_scores, k, (1, 0))
    grad_k = dot(d_scores, q, (0, 0))
    grad_v = dot(weights, d_out, (0, 0))
    return grad_q, grad_k, grad_v


def first_kernel(plan, place, held_ref, target_ref, halo_ref, gq_ref, gkv_ref, far_ref, ext, acc):
    seg = place[0]
    near = plan.reach * plan.rows
    for at in range(2):
        for head in range(plan.heads):
            for block in range(plan.reach):
                for part in range(plan.fold):
                    start = block * plan.rows + part * plan.fold_rows
                    ext[at, head, start : start + plan.fold_rows, :] = head_part(
                        halo_ref, (block, at), head, part, plan
                    )
            ext[at, head, near:, :] = held_ref[1 + at, head, :near, :]
    acc[...] = jnp.zeros_like(acc)

    def body(i, _):
        head, block = i // plan.reach, i % plan.reach
        start = pl.multiple_of(block * plan.rows, plan.rows)
        rows, keys = pl.ds(start, plan.rows), pl.ds(start, near + plan.rows)
        open_far = jnp.where(seg == 0, near - start, 0)
        gq, gk, gv = student_block(
            plan,
            held_ref[0, head, rows, :],
            ext[0, head, keys, :],
            ext[1, head, keys, :],
            target_ref[head, rows, :],
            open_far,
        )
        gq_ref[head, rows, :] = gq.astype(BF16)
        acc[0, head, keys, :] += gk
        acc[1, head, keys, :] += gv
        return 0

    lax.fori_loop(0, plan.heads * plan.reach, body, 0, unroll=2)
    gkv_ref[...] = acc[:, :, near:, :]
    for at in range(2):
        for block in range(plan.reach):
            for part in range(plan.fold):
                start = block * plan.rows + part * plan.fold_rows
                for head in range(plan.heads):
                    lane = part * plan.chunk_width + head * plan.dim
                    far_ref[block, at, :, lane : lane + plan.dim] = acc[
                        at, head, start : start + plan.fold_rows, :
                    ].astype(BF16)


def first_blocks(plan, place, held, target, halo):
    near = plan.reach * plan.rows
    outs = [
        shape((plan.heads, near, plan.dim)),
        shape((2, plan.heads, near, plan.dim), F32),
        shape((plan.reach, 2) + plan.piece),
    ]
    scratch = [
        pltpu.VMEM((2, plan.heads, 2 * near, plan.dim), BF16),
        pltpu.VMEM((2, plan.heads, 2 * near, plan.dim), F32),
    ]
    flops = 12 * plan.heads * near * (near + plan.rows) * plan.dim
    return call(
        functools.partial(first_kernel, plan), place, [held, target, halo], outs, scratch, flops
    )


def rest_kernel(plan, place, held_ref, target_ref, start_ref, gq_ref, acc):
    near = plan.reach * plan.rows
    acc[:, :, :near, :] = start_ref[...]
    acc[:, :, near:, :] = jnp.zeros((2, plan.heads, plan.seg_rows - near, plan.dim), F32)
    count = plan.devs - plan.reach

    def body(i, _):
        head, block = i // count, i % count
        start = pl.multiple_of(block * plan.rows, plan.rows)
        rows = pl.ds(pl.multiple_of(start + near, plan.rows), plan.rows)
        keys = pl.ds(start, near + plan.rows)
        gq, gk, gv = student_block(
            plan,
            held_ref[0, head, rows, :],
            held_ref[1, head, keys, :],
            held_ref[2, head, keys, :],
            target_ref[head, rows, :],
            None,
        )
        gq_ref[head, pl.ds(start, plan.rows), :] = gq.astype(BF16)
        acc[0, head, keys, :] += gk
        acc[1, head, keys, :] += gv
        return 0

    lax.fori_loop(0, plan.heads * count, body, 0, unroll=2)


def rest_blocks(plan, place, held, target, start):
    near = plan.reach * plan.rows
    outs = [
        shape((plan.heads, plan.seg_rows - near, plan.dim)),
        shape((2, plan.heads, plan.seg_rows, plan.dim), F32),
    ]
    flops = 12 * plan.heads * (plan.seg_rows - near) * (near + plan.rows) * plan.dim
    return call(
        functools.partial(rest_kernel, plan), place, [held, target, start], outs, (), flops
    )


def finish_kernel(plan, place, gq_first, gq_rest, gkv, far, *refs):
    me = place[1]
    out_refs, (grads,) = refs[: plan.devs], refs[plan.devs :]
    near = plan.reach * plan.rows
    last = plan.seg_rows - near
    for head in range(plan.heads):
        grads[0, head, :near, :] = gq_first[head]
        grads[0, head, near:, :] = gq_rest[head]
        for at in range(2):
            grads[1 + at, head, :last, :] = gkv[at, head, :last, :].astype(BF16)
            for block in range(plan.reach):
                for part in range(plan.fold):
                    start = last + block * plan.rows + part * plan.fold_rows
                    span = slice(start, start + plan.fold_rows)
                    back = head_part(far, (block, at), head, part, plan).astype(F32)
                    grads[1 + at, head, span, :] = (gkv[at, head, span, :] + back).astype(BF16)
    for step, out_ref in enumerate(out_refs):
        first = (me ^ step) * plan.rows
        for at in range(3):
            for part in range(plan.fold):
                start = pl.multiple_of(first + part * plan.fold_rows, plan.fold_rows)
                held = [
                    grads[at, head, pl.ds(start, plan.fold_rows), :] for head in range(plan.heads)
                ]
                lane = part * plan.chunk_width
                out_ref[at, :, lane : lane + plan.chunk_width] = (
                    held[0] if plan.heads == 1 else jnp.concatenate(held, axis=1)
                )


def finish(plan, place, gq_first, gq_rest, gkv, far):
    outs = [shape((3,) + plan.piece) for _ in range(plan.devs)]
    scratch = [pltpu.VMEM((3, plan.heads, plan.seg_rows, plan.dim), BF16)]
    arrays = [gq_first, gq_rest, gkv, far]
    return call(functools.partial(finish_kernel, plan), place, arrays, outs, scratch)


def local(queries, keys, values):
    rows, width = queries.shape
    plan = Plan(rows, width, lax.axis_size("dev"))
    seg_count = lax.axis_size("seg")
    onward = [(i, i + 1) for i in range(seg_count - 1)]
    backward = [(i + 1, i) for i in range(seg_count - 1)]
    me = lax.axis_index("dev")
    place = jnp.stack([lax.axis_index("seg"), me]).astype(jnp.int32)
    arrays = [queries, keys, values]
    arrays = [queries, keys, values]
    arrived = []
    for c in range(plan.chunks):
        pieces = pack(plan, c, place, arrays)
        arrived.append(exchange(plan, pieces))
    returned = []
    for pieces in arrived:
        halo = jnp.stack(
            [
                lax.select_n((plan.devs - plan.reach + b) ^ me, *[p[1:] for p in pieces])
                for b in range(plan.reach)
            ]
        )
        halo = lax.ppermute(halo, "seg", onward)
        held, target = teacher(plan, place, pieces)
        gq_first, gkv, far = first_blocks(plan, place, held, target, halo)
        far = lax.ppermute(far, "seg", backward)
        gq_rest, gkv = rest_blocks(plan, place, held, target, gkv)
        pieces = finish(plan, place, gq_first, gq_rest, gkv, far)
        returned.append(exchange(plan, pieces))
    return tuple(unpack(plan, place, returned))


def solution(mesh):
    spec = P(("seg", "dev"), None)
    return jax.shard_map(
        local, mesh=mesh, in_specs=(spec,) * 3, out_specs=(spec,) * 3, check_vma=False
    )
```

```python
import functools
import math

import jax
import jax.numpy as jnp
from jax import lax
from jax.experimental import pallas as pl
from jax.experimental.pallas import tpu as pltpu
from jax.sharding import PartitionSpec as P


HEADS = 16
WINDOW = 256
CHUNKS = 2
NEGATIVE = -1e30
LOG2E = math.log2(math.e)
BF16 = jnp.bfloat16
F32 = jnp.float32


SMEM_SPEC = pl.BlockSpec(memory_space=pltpu.SMEM)
VMEM_SPEC = pl.BlockSpec(memory_space=pltpu.VMEM)
HBM_SPEC = pl.BlockSpec(memory_space=pltpu.HBM)


def call(kernel, place, arrays, outs, scratch=(), flops=0, spec=VMEM_SPEC):
    moved = sum(a.size * a.dtype.itemsize for a in arrays)
    moved += sum(math.prod(o.shape) * o.dtype.itemsize for o in outs)
    return pl.pallas_call(
        kernel,
        out_shape=tuple(outs),
        in_specs=[SMEM_SPEC] + [spec] * len(arrays),
        out_specs=tuple([VMEM_SPEC] * len(outs)),
        scratch_shapes=list(scratch),
        cost_estimate=pl.CostEstimate(flops=flops, bytes_accessed=moved, transcendentals=0),
        compiler_params=pltpu.CompilerParams(vmem_limit_bytes=48 * 1024 * 1024),
    )(place, *arrays)


def shape(dims, dtype=BF16):
    return jax.ShapeDtypeStruct(dims, dtype)


class Plan:
    def __init__(self, rows, width, devs):
        self.rows, self.width, self.devs = rows, width, devs
        self.dim = width // HEADS
        self.local_heads = HEADS // devs
        self.local_width = width // devs
        self.chunks = CHUNKS if self.local_heads % CHUNKS == 0 else 1
        self.heads = self.local_heads // self.chunks
        self.chunk_width = self.heads * self.dim
        self.fold = 128 // math.gcd(self.chunk_width, 128)
        self.fold_rows = rows // self.fold
        self.piece = (self.fold_rows, self.fold * self.chunk_width)
        self.reach = WINDOW // rows
        self.seg_rows = rows * devs
        self.near = self.reach * rows
        self.groups = self.seg_rows // self.near
        self.teacher_rows = self.seg_rows if self.seg_rows <= 512 else rows
        self.scale = self.dim ** (-0.5)


def folded(x, plan):
    full = plan.chunk_width // 128 * 128
    parts = [x[i * plan.fold_rows : (i + 1) * plan.fold_rows] for i in range(plan.fold)]
    columns = [p[:, at : at + 128] for at in range(0, full, 128) for p in parts]
    if plan.chunk_width > full:
        columns += [p[:, full:] for p in parts]
    return columns[0] if len(columns) == 1 else jnp.concatenate(columns, axis=1)


def unfolded(x, plan):
    full = plan.chunk_width // 128 * 128
    rest = plan.chunk_width - full
    groups = []
    for i in range(plan.fold):
        columns = [
            x[:, at * plan.fold + i * 128 : at * plan.fold + (i + 1) * 128]
            for at in range(0, full, 128)
        ]
        if rest:
            start = plan.fold * full + i * rest
            columns.append(x[:, start : start + rest])
        groups.append(columns[0] if len(columns) == 1 else jnp.concatenate(columns, axis=1))
    return groups


def pack_kernel(plan, chunk, place, *refs):
    me = place[1]
    in_refs, out_refs = refs[:3], refs[3 : 3 + plan.devs]
    held, sems = refs[3 + plan.devs :]
    copies = [pltpu.make_async_copy(r, held.at[i], sems.at[i]) for i, r in enumerate(in_refs)]
    for copy in copies:
        copy.start()
    for at, copy in enumerate(copies):
        copy.wait()
        for step, out_ref in enumerate(out_refs):
            start = pl.multiple_of((me ^ step) * plan.local_width, 128)
            x = held[at, :, pl.ds(start, plan.local_width)]
            x = x[:, chunk * plan.chunk_width : (chunk + 1) * plan.chunk_width]
            out_ref[at] = folded(x, plan)


def pack(plan, chunk, place, arrays):
    if plan.local_width % 128 == 0:
        outs = [shape((3,) + plan.piece) for _ in range(plan.devs)]
        scratch = [
            pltpu.VMEM((3, plan.rows, plan.width), BF16),
            pltpu.SemaphoreType.DMA((3,)),
        ]
        kernel = functools.partial(pack_kernel, plan, chunk)
        return call(kernel, place, arrays, outs, scratch, spec=HBM_SPEC)
    pieces = []
    for step in range(plan.devs):
        start = (place[1] ^ step) * plan.local_width + chunk * plan.chunk_width
        taken = [lax.dynamic_slice_in_dim(a, start, plan.chunk_width, 1) for a in arrays]
        pieces.append(jnp.stack([folded(x, plan) for x in taken]))
    return pieces


def unpack_kernel(plan, place, *refs):
    me = place[1]
    piece_refs, out_refs = refs[:-3], refs[-3:]
    for step in range(plan.devs):
        start = pl.multiple_of((me ^ step) * plan.local_width, 128)
        for at, out_ref in enumerate(out_refs):
            held = [unfolded(piece_refs[c * plan.devs + step][at], plan) for c in range(plan.chunks)]
            for part in range(plan.fold):
                rows = slice(part * plan.fold_rows, (part + 1) * plan.fold_rows)
                x = [groups[part] for groups in held]
                out_ref[rows, pl.ds(start, plan.local_width)] = (
                    x[0] if plan.chunks == 1 else jnp.concatenate(x, axis=1)
                )


def unpack(plan, place, pieces):
    if plan.local_width % 128 == 0:
        flat = [piece for chunk in pieces for piece in chunk]
        outs = [shape((plan.rows, plan.width)) for _ in range(3)]
        return call(functools.partial(unpack_kernel, plan), place, flat, outs)
    order = jnp.arange(plan.devs, dtype=jnp.int32) ^ place[1]
    chunks = []
    for chunk in pieces:
        x = jnp.take(jnp.stack(chunk), order, axis=0)
        x = [jnp.concatenate(unfolded(x[d, at], plan), 0) for d in range(plan.devs) for at in range(3)]
        x = jnp.stack(x).reshape(plan.devs, 3, plan.rows, plan.chunk_width)
        chunks.append(x.transpose(1, 2, 0, 3))
    out = jnp.concatenate(chunks, axis=3).reshape(3, plan.rows, plan.width)
    return out[0], out[1], out[2]


def exchange(plan, pieces):
    got = [pieces[0]] + [None] * (plan.devs - 1)
    for step in range(plan.devs - 1, 0, -1):
        pairs = [(i, i ^ step) for i in range(plan.devs)]
        got[step] = lax.ppermute(pieces[step], "dev", pairs)
    return got


def dot(a, b, over):
    return lax.dot_general(a, b, ((over[:1], over[1:]), ((), ())), preferred_element_type=F32)


def of_head(x, head, plan):
    if plan.heads == 1:
        return x
    lane = lax.broadcasted_iota(jnp.int32, x.shape, 1)
    own = (lane >= head * plan.dim) & (lane < (head + 1) * plan.dim)
    return jnp.where(own, x, jnp.zeros_like(x))


def block_parts(first, plan):
    for part in range(plan.fold):
        start = first + part * plan.fold_rows
        yield part, pl.ds(pl.multiple_of(start, plan.fold_rows), plan.fold_rows)


def teacher_kernel(plan, place, *refs):
    me = place[1]
    piece_refs, (q_ref, k_ref, v_ref, target_ref) = refs[: plan.devs], refs[plan.devs :]
    for step, ref in enumerate(piece_refs):
        blocks = [unfolded(ref[at], plan) for at in range(3)]
        for part, rows in block_parts((me ^ step) * plan.rows, plan):
            q_ref[rows, :] = blocks[0][part]
            for head in range(plan.heads):
                k_ref[head, rows, :] = of_head(blocks[1][part], head, plan)
                v_ref[head, rows, :] = of_head(blocks[2][part], head, plan)

    def one(start, count):
        rows = pl.ds(start, count)
        total = None
        for head in range(plan.heads):
            scores = dot(q_ref[rows, :], k_ref[head], (1, 1))
            top = scores.max(-1, keepdims=True)
            e = jnp.exp2((scores - top) * (plan.scale * LOG2E))
            out = dot(e.astype(BF16), v_ref[head], (1, 0)) / e.sum(-1, keepdims=True)
            total = out if total is None else total + out
        target_ref[rows, :] = total.astype(BF16)

    count = plan.teacher_rows
    if count == plan.seg_rows:
        one(0, count)
    else:

        def body(i, _):
            one(pl.multiple_of(i * count, count), count)
            return 0

        lax.fori_loop(0, plan.seg_rows // count, body, 0)


def teacher(plan, place, pieces):
    outs = [
        shape((plan.seg_rows, plan.chunk_width)),
        shape((plan.heads, plan.seg_rows, plan.chunk_width)),
        shape((plan.heads, plan.seg_rows, plan.chunk_width)),
        shape((plan.seg_rows, plan.chunk_width)),
    ]
    flops = 4 * plan.heads * plan.seg_rows * plan.seg_rows * plan.dim
    return call(functools.partial(teacher_kernel, plan), place, list(pieces), outs, flops=flops)


def student_group(plan, q, k, v, target, closed):
    heads = range(plan.heads)
    weights, probability = [], []
    out = None
    for head in heads:
        scores = dot(q, k[head], (1, 1))
        query_at = lax.broadcasted_iota(jnp.int32, scores.shape, 0)
        key_at = lax.broadcasted_iota(jnp.int32, scores.shape, 1)
        low = query_at if closed is None else jnp.maximum(query_at, closed)
        allowed = (key_at >= low) & (key_at <= query_at + plan.near)
        scores = jnp.where(allowed, scores, NEGATIVE)
        top = scores.max(-1, keepdims=True)
        e = jnp.exp2((scores - top) * (plan.scale * LOG2E))
        p = e * (1.0 / e.sum(-1, keepdims=True))
        probability.append(p)
        weights.append(p.astype(BF16))
        part = dot(weights[head], v[head], (1, 0))
        out = part if out is None else out + part
    d_out = (128.0 * (out - target.astype(F32))).astype(BF16)
    gq = gk = gv = None
    for head in heads:
        d_prob = dot(d_out, v[head], (1, 1))
        p = probability[head]
        inner = (p * d_prob).sum(-1, keepdims=True)
        d_scores = (p * (d_prob - inner) * plan.scale).astype(BF16)
        parts = (
            dot(d_scores, k[head], (1, 0)),
            dot(d_scores, of_head(q, head, plan), (0, 0)),
            dot(weights[head], of_head(d_out, head, plan), (0, 0)),
        )
        gq, gk, gv = parts if gq is None else (gq + parts[0], gk + parts[1], gv + parts[2])
    return gq, gk, gv


def first_kernel(
    plan, place, q_ref, k_ref, v_ref, target_ref, halo_ref, gq_ref, gk_ref, gv_ref, far_ref, ext
):
    near, heads = plan.near, range(plan.heads)
    for at, ref in enumerate((k_ref, v_ref)):
        for block in range(plan.reach):
            groups = unfolded(halo_ref[block, at], plan)
            for part, rows in block_parts(block * plan.rows, plan):
                for head in heads:
                    ext[at, head, rows, :] = of_head(groups[part], head, plan)
        for head in heads:
            ext[at, head, near:, :] = ref[head, :near, :]
    gq, gk, gv = student_group(
        plan,
        q_ref[:near, :],
        [ext[0, head] for head in heads],
        [ext[1, head] for head in heads],
        target_ref[:near, :],
        jnp.where(place[0] == 0, near, 0),
    )
    gq_ref[...] = gq.astype(BF16)
    for at, (grad, ref) in enumerate(((gk, gk_ref), (gv, gv_ref))):
        ref[...] = grad[near:]
        for block in range(plan.reach):
            rows = slice(block * plan.rows, (block + 1) * plan.rows)
            far_ref[block, at] = folded(grad[rows].astype(BF16), plan)


def first_group(plan, place, held, halo):
    near = plan.near
    outs = [
        shape((near, plan.chunk_width)),
        shape((near, plan.chunk_width), F32),
        shape((near, plan.chunk_width), F32),
        shape((plan.reach, 2) + plan.piece),
    ]
    scratch = [pltpu.VMEM((2, plan.heads, 2 * near, plan.chunk_width), BF16)]
    flops = 24 * plan.heads * near * near * plan.dim
    kernel = functools.partial(first_kernel, plan)
    return call(kernel, place, list(held) + [halo], outs, scratch, flops)


def rest_kernel(
    plan, place, q_ref, k_ref, v_ref, target_ref, k_start, v_start, gq_ref, gk_ref, gv_ref
):
    near, heads = plan.near, range(plan.heads)

    def group(start):
        rows, keys = pl.ds(start + near, near), pl.ds(start, 2 * near)
        return student_group(
            plan,
            q_ref[rows, :],
            [k_ref[head, keys, :] for head in heads],
            [v_ref[head, keys, :] for head in heads],
            target_ref[rows, :],
            None,
        )

    if plan.groups == 2:
        gq, gk, gv = group(0)
        gq_ref[...] = gq.astype(BF16)
        for grad, start, ref in ((gk, k_start, gk_ref), (gv, v_start, gv_ref)):
            ref[:near, :] = grad[:near] + start[...]
            ref[near:, :] = grad[near:]
        return
    for start, ref in ((k_start, gk_ref), (v_start, gv_ref)):
        ref[:near, :] = start[...]
        ref[near:, :] = jnp.zeros((plan.seg_rows - near, plan.chunk_width), F32)

    def body(i, _):
        start = pl.multiple_of(i * near, near)
        gq, gk, gv = group(start)
        gq_ref[pl.ds(start, near), :] = gq.astype(BF16)
        gk_ref[pl.ds(start, 2 * near), :] += gk
        gv_ref[pl.ds(start, 2 * near), :] += gv
        return 0

    lax.fori_loop(0, plan.groups - 1, body, 0)


def rest_groups(plan, place, held, starts):
    near = plan.near
    outs = [
        shape((plan.seg_rows - near, plan.chunk_width)),
        shape((plan.seg_rows, plan.chunk_width), F32),
        shape((plan.seg_rows, plan.chunk_width), F32),
    ]
    flops = 24 * plan.heads * (plan.seg_rows - near) * near * plan.dim
    kernel = functools.partial(rest_kernel, plan)
    return call(kernel, place, list(held) + list(starts), outs, (), flops)


def finish_kernel(plan, place, gq_first, gq_rest, gk, gv, far, *refs):
    me = place[1]
    out_refs, (grads,) = refs[: plan.devs], refs[plan.devs :]
    near = plan.near
    last = plan.seg_rows - near
    grads[0, :near, :] = gq_first[...]
    grads[0, near:, :] = gq_rest[...]
    for at, ref in enumerate((gk, gv)):
        grads[1 + at, :last, :] = ref[:last, :].astype(BF16)
        for block in range(plan.reach):
            groups = unfolded(far[block, at], plan)
            for part, rows in block_parts(last + block * plan.rows, plan):
                grads[1 + at, rows, :] = (ref[rows, :] + groups[part].astype(F32)).astype(BF16)
    for step, out_ref in enumerate(out_refs):
        rows = pl.ds(pl.multiple_of((me ^ step) * plan.rows, plan.rows), plan.rows)
        for at in range(3):
            out_ref[at] = folded(grads[at, rows, :], plan)


def finish(plan, place, gq_first, gq_rest, gk, gv, far):
    outs = [shape((3,) + plan.piece) for _ in range(plan.devs)]
    scratch = [pltpu.VMEM((3, plan.seg_rows, plan.chunk_width), BF16)]
    arrays = [gq_first, gq_rest, gk, gv, far]
    return call(functools.partial(finish_kernel, plan), place, arrays, outs, scratch)


def local(queries, keys, values):
    rows, width = queries.shape
    plan = Plan(rows, width, lax.axis_size("dev"))
    seg_count = lax.axis_size("seg")
    onward = [(i, i + 1) for i in range(seg_count - 1)]
    backward = [(i + 1, i) for i in range(seg_count - 1)]
    me = lax.axis_index("dev")
    place = jnp.stack([lax.axis_index("seg"), me]).astype(jnp.int32)
    arrays = [queries, keys, values]
    arrays = [queries, keys, values]
    arrived = []
    for c in range(plan.chunks):
        pieces = pack(plan, c, place, arrays)
        arrived.append(exchange(plan, pieces))
    returned = []
    for pieces in arrived:
        halo = jnp.stack(
            [
                lax.select_n((plan.devs - plan.reach + b) ^ me, *[p[1:] for p in pieces])
                for b in range(plan.reach)
            ]
        )
        halo = lax.ppermute(halo, "seg", onward)
        held = teacher(plan, place, pieces)
        gq_first, gk, gv, far = first_group(plan, place, held, halo)
        far = lax.ppermute(far, "seg", backward)
        gq_rest, gk, gv = rest_groups(plan, place, held, (gk, gv))
        pieces = finish(plan, place, gq_first, gq_rest, gk, gv, far)
        returned.append(exchange(plan, pieces))
    return tuple(unpack(plan, place, returned))


def solution(mesh):
    spec = P(("seg", "dev"), None)
    return jax.shard_map(
        local, mesh=mesh, in_specs=(spec,) * 3, out_specs=(spec,) * 3, check_vma=False
    )
```

```python
import functools
import math

import jax
import jax.numpy as jnp
from jax import lax
from jax.experimental import pallas as pl
from jax.experimental.pallas import tpu as pltpu
from jax.sharding import PartitionSpec as P


HEADS = 16
WINDOW = 256
CHUNKS = 2
PACK_MIB = 58
NEGATIVE = -1e30
LOG2E = math.log2(math.e)
BF16 = jnp.bfloat16
F32 = jnp.float32


SMEM_SPEC = pl.BlockSpec(memory_space=pltpu.SMEM)
VMEM_SPEC = pl.BlockSpec(memory_space=pltpu.VMEM)
HBM_SPEC = pl.BlockSpec(memory_space=pltpu.HBM)


def call(kernel, place, arrays, outs, scratch=(), flops=0, spec=VMEM_SPEC, out_spec=VMEM_SPEC, vmem=48):
    moved = sum(a.size * a.dtype.itemsize for a in arrays)
    moved += sum(math.prod(o.shape) * o.dtype.itemsize for o in outs)
    return pl.pallas_call(
        kernel,
        out_shape=tuple(outs),
        in_specs=[SMEM_SPEC] + [spec] * len(arrays),
        out_specs=tuple([out_spec] * len(outs)),
        scratch_shapes=list(scratch),
        cost_estimate=pl.CostEstimate(flops=flops, bytes_accessed=moved, transcendentals=0),
        compiler_params=pltpu.CompilerParams(vmem_limit_bytes=vmem * 1024 * 1024),
    )(place, *arrays)


def shape(dims, dtype=BF16):
    return jax.ShapeDtypeStruct(dims, dtype)


class Plan:
    def __init__(self, rows, width, devs):
        self.rows, self.width, self.devs = rows, width, devs
        self.dim = width // HEADS
        self.local_heads = HEADS // devs
        self.local_width = width // devs
        self.chunks = CHUNKS if self.local_heads % CHUNKS == 0 else 1
        self.heads = self.local_heads // self.chunks
        self.chunk_width = self.heads * self.dim
        self.fold = 128 // math.gcd(self.chunk_width, 128)
        self.fold_rows = rows // self.fold
        self.piece = (self.fold_rows, self.fold * self.chunk_width)
        self.reach = WINDOW // rows
        self.seg_rows = rows * devs
        self.near = self.reach * rows
        self.groups = self.seg_rows // self.near
        self.scale = self.dim ** (-0.5)


def folded(x, plan):
    full = plan.chunk_width // 128 * 128
    parts = [x[i * plan.fold_rows : (i + 1) * plan.fold_rows] for i in range(plan.fold)]
    columns = [p[:, at : at + 128] for at in range(0, full, 128) for p in parts]
    if plan.chunk_width > full:
        columns += [p[:, full:] for p in parts]
    return columns[0] if len(columns) == 1 else jnp.concatenate(columns, axis=1)


def unfolded(x, plan):
    full = plan.chunk_width // 128 * 128
    rest = plan.chunk_width - full
    groups = []
    for i in range(plan.fold):
        columns = [
            x[:, at * plan.fold + i * 128 : at * plan.fold + (i + 1) * 128]
            for at in range(0, full, 128)
        ]
        if rest:
            start = plan.fold * full + i * rest
            columns.append(x[:, start : start + rest])
        groups.append(columns[0] if len(columns) == 1 else jnp.concatenate(columns, axis=1))
    return groups


def pack_kernel(plan, chunk, place, *refs):
    me = place[1]
    in_refs, out_refs, (held, sems) = refs[:3], refs[3:-2], refs[-2:]
    copies = [pltpu.make_async_copy(r, held.at[i], sems.at[i]) for i, r in enumerate(in_refs)]
    for copy in copies:
        copy.start()
    for at, copy in enumerate(copies):
        copy.wait()
        for step, out_ref in enumerate(out_refs):
            start = pl.multiple_of((me ^ step) * plan.local_width, 128)
            x = held[at, :, pl.ds(start, plan.local_width)]
            x = x[:, chunk * plan.chunk_width : (chunk + 1) * plan.chunk_width]
            out_ref[at] = folded(x, plan)


def pack(plan, chunk, place, arrays):
    if plan.local_width % 128 == 0:
        outs = [shape((3,) + plan.piece) for _ in range(plan.devs)]
        kernel = functools.partial(pack_kernel, plan, chunk)
        scratch = [
            pltpu.VMEM((3, plan.rows, plan.width), BF16),
            pltpu.SemaphoreType.DMA((3,)),
        ]
        vmem = PACK_MIB if chunk == 0 else 48
        return call(kernel, place, arrays, outs, scratch, spec=HBM_SPEC, vmem=vmem)
    pieces = []
    for step in range(plan.devs):
        start = (place[1] ^ step) * plan.local_width + chunk * plan.chunk_width
        taken = [lax.dynamic_slice_in_dim(a, start, plan.chunk_width, 1) for a in arrays]
        pieces.append(jnp.stack([folded(x, plan) for x in taken]))
    return pieces


def unpack_kernel(plan, place, *refs):
    me = place[1]
    piece_refs, out_refs, (held, sems) = refs[:-5], refs[-5:-2], refs[-2:]
    copies = [pltpu.make_async_copy(held.at[i], r, sems.at[i]) for i, r in enumerate(out_refs)]
    for at in range(3):
        for step in range(plan.devs):
            start = pl.multiple_of((me ^ step) * plan.local_width, 128)
            got = [unfolded(piece_refs[c * plan.devs + step][at], plan) for c in range(plan.chunks)]
            for part in range(plan.fold):
                rows = slice(part * plan.fold_rows, (part + 1) * plan.fold_rows)
                x = [groups[part] for groups in got]
                held[at, rows, pl.ds(start, plan.local_width)] = (
                    x[0] if plan.chunks == 1 else jnp.concatenate(x, axis=1)
                )
        copies[at].start()
    for copy in copies:
        copy.wait()


def unpack(plan, place, pieces):
    if plan.local_width % 128 == 0:
        flat = [piece for chunk in pieces for piece in chunk]
        outs = [shape((plan.rows, plan.width)) for _ in range(3)]
        scratch = [
            pltpu.VMEM((3, plan.rows, plan.width), BF16),
            pltpu.SemaphoreType.DMA((3,)),
        ]
        kernel = functools.partial(unpack_kernel, plan)
        return call(kernel, place, flat, outs, scratch, out_spec=HBM_SPEC)
    order = jnp.arange(plan.devs, dtype=jnp.int32) ^ place[1]
    chunks = []
    for chunk in pieces:
        x = jnp.take(jnp.stack(chunk), order, axis=0)
        x = [jnp.concatenate(unfolded(x[d, at], plan), 0) for d in range(plan.devs) for at in range(3)]
        x = jnp.stack(x).reshape(plan.devs, 3, plan.rows, plan.chunk_width)
        chunks.append(x.transpose(1, 2, 0, 3))
    out = jnp.concatenate(chunks, axis=3).reshape(3, plan.rows, plan.width)
    return out[0], out[1], out[2]


def exchange(plan, pieces):
    got = [pieces[0]] + [None] * (plan.devs - 1)
    for step in range(plan.devs - 1, 0, -1):
        pairs = [(i, i ^ step) for i in range(plan.devs)]
        got[step] = lax.ppermute(pieces[step], "dev", pairs)
    return got


def dot(a, b, over):
    return lax.dot_general(a, b, ((over[:1], over[1:]), ((), ())), preferred_element_type=F32)


def of_head(x, head, plan):
    if plan.heads == 1:
        return x
    lane = lax.broadcasted_iota(jnp.int32, x.shape, 1)
    own = (lane >= head * plan.dim) & (lane < (head + 1) * plan.dim)
    return jnp.where(own, x, jnp.zeros_like(x))


def joined(parts, plan):
    columns = []
    for first in range(0, plan.chunk_width, 128):
        end = min(first + 128, plan.chunk_width)
        out = None
        for head in range(plan.heads):
            if head * plan.dim >= end or (head + 1) * plan.dim <= first:
                continue
            x = parts[head][:, first:end]
            if out is None:
                out = x
            else:
                lane = first + lax.broadcasted_iota(jnp.int32, x.shape, 1)
                out = jnp.where(lane < head * plan.dim, out, x)
        columns.append(out)
    return columns[0] if len(columns) == 1 else jnp.concatenate(columns, axis=1)


def block_parts(first, plan):
    for part in range(plan.fold):
        start = first + part * plan.fold_rows
        yield part, pl.ds(pl.multiple_of(start, plan.fold_rows), plan.fold_rows)


def teacher_rows(plan, q, k, v):
    parts = []
    for head in range(plan.heads):
        scores = dot(of_head(q, head, plan), k, (1, 1))
        top = scores.max(-1, keepdims=True)
        e = jnp.exp2((scores - top) * (plan.scale * LOG2E))
        parts.append(dot(e.astype(BF16), v, (1, 0)) * (1.0 / e.sum(-1, keepdims=True)))
    return joined(parts, plan).astype(BF16)


def student_group(plan, q, k, v, target, open_far):
    rows, reach, heads = plan.rows, plan.reach, range(plan.heads)
    at_query = lax.broadcasted_iota(jnp.int32, (rows, rows), 0)
    at_key = lax.broadcasted_iota(jnp.int32, (rows, rows), 1)
    late, early = at_key >= at_query, at_key <= at_query

    def seen(i, block, j):
        mask = None
        if j == i:
            mask = late
        elif j == i + reach:
            mask = early
        if open_far is not None and j < reach:
            mask = jnp.broadcast_to(open_far, (rows, rows)) if mask is None else mask & open_far
        return block if mask is None else jnp.where(mask, block, NEGATIVE)

    def window(x, i):
        return x[i * rows : (i + 1) * rows, i * rows : (i + reach + 1) * rows]

    def whole(parts):
        lines = []
        for i, x in enumerate(parts):
            left = [jnp.zeros((rows, i * rows), x.dtype)] if i else []
            right = [jnp.zeros((rows, (reach - 1 - i) * rows), x.dtype)] if i < reach - 1 else []
            lines.append(jnp.concatenate(left + [x] + right, axis=1))
        return lines[0] if reach == 1 else jnp.concatenate(lines, axis=0)

    weights, probability, outs = [], [], []
    for head in heads:
        scores = dot(of_head(q, head, plan), k, (1, 1))
        ps = []
        for i in range(reach):
            s = window(scores, i)
            s = [seen(i, s[:, j * rows : (j + 1) * rows], i + j) for j in range(reach + 1)]
            s = jnp.concatenate(s, axis=1)
            top = s.max(-1, keepdims=True)
            e = jnp.exp2((s - top) * (plan.scale * LOG2E))
            ps.append(e * (1.0 / e.sum(-1, keepdims=True)))
        probability.append(ps)
        weights.append(whole([p.astype(BF16) for p in ps]))
        outs.append(dot(weights[head], v, (1, 0)))
    d_out = (128.0 * (joined(outs, plan) - target.astype(F32))).astype(BF16)
    gq, gk, gv = [], [], []
    for head in heads:
        d_prob = dot(of_head(d_out, head, plan), v, (1, 1))
        ds = []
        for i, p in enumerate(probability[head]):
            d = window(d_prob, i)
            inner = (p * d).sum(-1, keepdims=True)
            ds.append((p * (d - inner) * plan.scale).astype(BF16))
        d_scores = whole(ds)
        gq.append(dot(d_scores, k, (1, 0)))
        gk.append(dot(d_scores, q, (0, 0)))
        gv.append(dot(weights[head], d_out, (0, 0)))
    return joined(gq, plan), joined(gk, plan), joined(gv, plan)


def first_kernel(plan, place, *refs):
    me, near = place[1], plan.near
    piece_refs, halo_ref = refs[: plan.devs], refs[plan.devs]
    q_ref, k_ref, v_ref, gq_ref, gk_ref, gv_ref, far_ref, ext = refs[plan.devs + 1 :]
    for step, ref in enumerate(piece_refs):
        for at, to in enumerate((q_ref, k_ref, v_ref)):
            groups = unfolded(ref[at], plan)
            for part, rows in block_parts((me ^ step) * plan.rows, plan):
                to[rows, :] = groups[part]
    target = teacher_rows(plan, q_ref[:near, :], k_ref[...], v_ref[...])
    for at, ref in enumerate((k_ref, v_ref)):
        for block in range(plan.reach):
            groups = unfolded(halo_ref[block, at], plan)
            for part, rows in block_parts(block * plan.rows, plan):
                ext[at, rows, :] = groups[part]
        ext[at, near:, :] = ref[:near, :]
    gq, gk, gv = student_group(plan, q_ref[:near, :], ext[0], ext[1], target, place[0] > 0)
    gq_ref[...] = gq.astype(BF16)
    for at, (grad, ref) in enumerate(((gk, gk_ref), (gv, gv_ref))):
        ref[...] = grad[near:]
        for block in range(plan.reach):
            rows = slice(block * plan.rows, (block + 1) * plan.rows)
            far_ref[block, at] = folded(grad[rows].astype(BF16), plan)


def first_group(plan, place, pieces, halo):
    near, width = plan.near, plan.chunk_width
    outs = [shape((plan.seg_rows, width))] * 3 + [
        shape((near, width)),
        shape((near, width), F32),
        shape((near, width), F32),
        shape((plan.reach, 2) + plan.piece),
    ]
    scratch = [pltpu.VMEM((2, 2 * near, width), BF16)]
    flops = plan.heads * near * plan.dim * (24 * near + 4 * plan.seg_rows)
    kernel = functools.partial(first_kernel, plan)
    out = call(kernel, place, list(pieces) + [halo], outs, scratch, flops)
    return out[:3], out[3:]


def rest_kernel(plan, place, q_ref, k_ref, v_ref, k_start, v_start, gq_ref, gk_ref, gv_ref):
    near = plan.near

    def group(start):
        rows, keys = pl.ds(start + near, near), pl.ds(start, 2 * near)
        q = q_ref[rows, :]
        target = teacher_rows(plan, q, k_ref[...], v_ref[...])
        return student_group(plan, q, k_ref[keys, :], v_ref[keys, :], target, None)

    if plan.groups == 2:
        gq, gk, gv = group(0)
        gq_ref[...] = gq.astype(BF16)
        for grad, start, ref in ((gk, k_start, gk_ref), (gv, v_start, gv_ref)):
            ref[:near, :] = grad[:near] + start[...]
            ref[near:, :] = grad[near:]
        return
    for start, ref in ((k_start, gk_ref), (v_start, gv_ref)):
        ref[:near, :] = start[...]
        ref[near:, :] = jnp.zeros((plan.seg_rows - near, plan.chunk_width), F32)

    def body(i, _):
        start = pl.multiple_of(i * near, near)
        gq, gk, gv = group(start)
        gq_ref[pl.ds(start, near), :] = gq.astype(BF16)
        gk_ref[pl.ds(start, 2 * near), :] += gk
        gv_ref[pl.ds(start, 2 * near), :] += gv
        return 0

    lax.fori_loop(0, plan.groups - 1, body, 0)


def rest_groups(plan, place, held, starts):
    near, width = plan.near, plan.chunk_width
    outs = [
        shape((plan.seg_rows - near, width)),
        shape((plan.seg_rows, width), F32),
        shape((plan.seg_rows, width), F32),
    ]
    count = plan.seg_rows - near
    flops = plan.heads * count * plan.dim * (24 * near + 4 * plan.seg_rows)
    kernel = functools.partial(rest_kernel, plan)
    return call(kernel, place, list(held) + list(starts), outs, (), flops)


def finish_kernel(plan, place, gq_first, gq_rest, gk, gv, far, *refs):
    me = place[1]
    out_refs, (grads,) = refs[: plan.devs], refs[plan.devs :]
    near = plan.near
    last = plan.seg_rows - near
    grads[0, :near, :] = gq_first[...]
    grads[0, near:, :] = gq_rest[...]
    for at, ref in enumerate((gk, gv)):
        grads[1 + at, :last, :] = ref[:last, :].astype(BF16)
        for block in range(plan.reach):
            groups = unfolded(far[block, at], plan)
            for part, rows in block_parts(last + block * plan.rows, plan):
                grads[1 + at, rows, :] = (ref[rows, :] + groups[part].astype(F32)).astype(BF16)
    for step, out_ref in enumerate(out_refs):
        rows = pl.ds(pl.multiple_of((me ^ step) * plan.rows, plan.rows), plan.rows)
        for at in range(3):
            out_ref[at] = folded(grads[at, rows, :], plan)


def finish(plan, place, gq_first, gq_rest, gk, gv, far):
    outs = [shape((3,) + plan.piece) for _ in range(plan.devs)]
    scratch = [pltpu.VMEM((3, plan.seg_rows, plan.chunk_width), BF16)]
    arrays = [gq_first, gq_rest, gk, gv, far]
    return call(functools.partial(finish_kernel, plan), place, arrays, outs, scratch)


def local(queries, keys, values):
    rows, width = queries.shape
    plan = Plan(rows, width, lax.axis_size("dev"))
    seg_count = lax.axis_size("seg")
    onward = [(i, i + 1) for i in range(seg_count - 1)]
    backward = [(i + 1, i) for i in range(seg_count - 1)]
    me = lax.axis_index("dev")
    place = jnp.stack([lax.axis_index("seg"), me]).astype(jnp.int32)
    arrays = [queries, keys, values]
    arrays = [queries, keys, values]
    arrived = []
    for c in range(plan.chunks):
        pieces = pack(plan, c, place, arrays)
        arrived.append(exchange(plan, pieces))
    returned = []
    for pieces in arrived:
        halo = jnp.stack(
            [
                lax.select_n((plan.devs - plan.reach + b) ^ me, *[p[1:] for p in pieces])
                for b in range(plan.reach)
            ]
        )
        halo = lax.ppermute(halo, "seg", onward)
        held, (gq_first, gk, gv, far) = first_group(plan, place, pieces, halo)
        far = lax.ppermute(far, "seg", backward)
        gq_rest, gk, gv = rest_groups(plan, place, held, (gk, gv))
        pieces = finish(plan, place, gq_first, gq_rest, gk, gv, far)
        returned.append(exchange(plan, pieces))
    return tuple(unpack(plan, place, returned))


def solution(mesh):
    spec = P(("seg", "dev"), None)
    return jax.shard_map(
        local, mesh=mesh, in_specs=(spec,) * 3, out_specs=(spec,) * 3, check_vma=False
    )
```

```python
import functools
import math

import jax
import jax.numpy as jnp
from jax import lax
from jax.experimental import pallas as pl
from jax.experimental.pallas import tpu as pltpu
from jax.sharding import PartitionSpec as P


HEADS = 16
WINDOW = 256
CHUNKS = 2
PACK_MIB = 58
NEGATIVE = -1e30
LOG2E = math.log2(math.e)
BF16 = jnp.bfloat16
F32 = jnp.float32


VMEM_SPEC = pl.BlockSpec(memory_space=pltpu.VMEM)
HBM_SPEC = pl.BlockSpec(memory_space=pltpu.HBM)


def call(kernel, arrays, outs, scratch=(), flops=0, spec=VMEM_SPEC, out_spec=VMEM_SPEC, vmem=48):
    moved = sum(a.size * a.dtype.itemsize for a in arrays)
    moved += sum(math.prod(o.shape) * o.dtype.itemsize for o in outs)
    return pl.pallas_call(
        kernel,
        out_shape=tuple(outs),
        in_specs=[spec] * len(arrays),
        out_specs=tuple([out_spec] * len(outs)),
        scratch_shapes=list(scratch),
        cost_estimate=pl.CostEstimate(flops=flops, bytes_accessed=moved, transcendentals=0),
        compiler_params=pltpu.CompilerParams(vmem_limit_bytes=vmem * 1024 * 1024),
    )(*arrays)


def shape(dims, dtype=BF16):
    return jax.ShapeDtypeStruct(dims, dtype)


class Plan:
    def __init__(self, rows, width, devs):
        self.rows, self.width, self.devs = rows, width, devs
        self.dim = width // HEADS
        self.local_heads = HEADS // devs
        self.local_width = width // devs
        self.chunks = CHUNKS if self.local_heads % CHUNKS == 0 else 1
        self.heads = self.local_heads // self.chunks
        self.chunk_width = self.heads * self.dim
        self.fold = 128 // math.gcd(self.chunk_width, 128)
        self.fold_rows = rows // self.fold
        self.piece = (self.fold_rows, self.fold * self.chunk_width)
        self.reach = WINDOW // rows
        self.seg_rows = rows * devs
        self.near = self.reach * rows
        self.groups = self.seg_rows // self.near
        self.teacher_rows = self.seg_rows if self.seg_rows <= 512 else rows
        self.scale = self.dim ** (-0.5)


def folded(x, plan):
    full = plan.chunk_width // 128 * 128
    parts = [x[i * plan.fold_rows : (i + 1) * plan.fold_rows] for i in range(plan.fold)]
    columns = [p[:, at : at + 128] for at in range(0, full, 128) for p in parts]
    if plan.chunk_width > full:
        columns += [p[:, full:] for p in parts]
    return columns[0] if len(columns) == 1 else jnp.concatenate(columns, axis=1)


def unfolded(x, plan):
    full = plan.chunk_width // 128 * 128
    rest = plan.chunk_width - full
    groups = []
    for i in range(plan.fold):
        columns = [
            x[:, at * plan.fold + i * 128 : at * plan.fold + (i + 1) * 128]
            for at in range(0, full, 128)
        ]
        if rest:
            start = plan.fold * full + i * rest
            columns.append(x[:, start : start + rest])
        groups.append(columns[0] if len(columns) == 1 else jnp.concatenate(columns, axis=1))
    return groups


def columns_of(x, chunk, plan):
    return folded(x[:, chunk * plan.chunk_width : (chunk + 1) * plan.chunk_width], plan)


def pack_first_kernel(plan, *refs):
    me = lax.axis_index("dev")
    in_refs, out_refs, (held, made, in_sems, out_sems) = refs[:3], refs[3:-4], refs[-4:]
    steps = range(plan.devs - 1, 0, -1)

    def taken(step, at):
        start = pl.multiple_of((me ^ step) * plan.local_width, 128)
        block = in_refs[at].at[:, pl.ds(start, plan.local_width)]
        return pltpu.make_async_copy(block, held.at[step - 1, at], in_sems.at[step - 1, at])

    def given(step):
        return pltpu.make_async_copy(
            made.at[step - 1], out_refs[step - 1], out_sems.at[step - 1]
        )

    for step in steps:
        for at in range(3):
            taken(step, at).start()
    for step in steps:
        for at in range(3):
            taken(step, at).wait()
            made[step - 1, at] = columns_of(held[step - 1, at], 0, plan)
        given(step).start()
    for step in steps:
        given(step).wait()


def pack_rest_kernel(plan, chunk, *refs):
    me = lax.axis_index("dev")
    in_refs, out_refs = refs[:3], refs[3:]
    for at in range(3):
        for step in range(plan.devs):
            start = pl.multiple_of((me ^ step) * plan.local_width, 128)
            x = in_refs[at][:, pl.ds(start, plan.local_width)]
            out_refs[step][at] = columns_of(x, chunk, plan)
            if chunk == 1 and step == 0:
                out_refs[plan.devs][at] = columns_of(x, 0, plan)


def pack(plan, arrays):
    piece = shape((3,) + plan.piece)
    chunks = []
    if plan.local_width % 128 == 0 and plan.chunks > 1:
        others = plan.devs - 1
        scratch = [
            pltpu.VMEM((others, 3, plan.rows, plan.local_width), BF16),
            pltpu.VMEM((others, 3) + plan.piece, BF16),
            pltpu.SemaphoreType.DMA((others, 3)),
            pltpu.SemaphoreType.DMA((others,)),
        ]
        kernel = functools.partial(pack_first_kernel, plan)
        sent = call(
            kernel, arrays, [piece] * others, scratch, spec=HBM_SPEC, out_spec=HBM_SPEC, vmem=PACK_MIB
        )
        chunks.append([None] + list(sent))
        for chunk in range(1, plan.chunks):
            kernel = functools.partial(pack_rest_kernel, plan, chunk)
            got = list(call(kernel, arrays, [piece] * (plan.devs + (chunk == 1))))
            if chunk == 1:
                chunks[0][0] = got.pop()
            chunks.append(got)
        return chunks
    me = lax.axis_index("dev")
    for chunk in range(plan.chunks):
        pieces = []
        for step in range(plan.devs):
            start = (me ^ step) * plan.local_width + chunk * plan.chunk_width
            taken = [lax.dynamic_slice_in_dim(a, start, plan.chunk_width, 1) for a in arrays]
            pieces.append(jnp.stack([folded(x, plan) for x in taken]))
        chunks.append(pieces)
    return chunks


def unpack_kernel(plan, *refs):
    me = lax.axis_index("dev")
    piece_refs, out_refs, (held, sems) = refs[:-5], refs[-5:-2], refs[-2:]

    def given(step, at):
        start = pl.multiple_of((me ^ step) * plan.local_width, 128)
        block = out_refs[at].at[:, pl.ds(start, plan.local_width)]
        return pltpu.make_async_copy(held.at[step, at], block, sems.at[step, at])

    for step in range(plan.devs):
        for at in range(3):
            got = [unfolded(piece_refs[c * plan.devs + step][at], plan) for c in range(plan.chunks)]
            for part in range(plan.fold):
                rows = slice(part * plan.fold_rows, (part + 1) * plan.fold_rows)
                x = [groups[part] for groups in got]
                held[step, at, rows, :] = x[0] if plan.chunks == 1 else jnp.concatenate(x, axis=1)
            given(step, at).start()
    for step in range(plan.devs):
        for at in range(3):
            given(step, at).wait()


def unpack(plan, pieces):
    if plan.local_width % 128 == 0:
        flat = [piece for chunk in pieces for piece in chunk]
        outs = [shape((plan.rows, plan.width)) for _ in range(3)]
        scratch = [
            pltpu.VMEM((plan.devs, 3, plan.rows, plan.local_width), BF16),
            pltpu.SemaphoreType.DMA((plan.devs, 3)),
        ]
        kernel = functools.partial(unpack_kernel, plan)
        return call(kernel, flat, outs, scratch, out_spec=HBM_SPEC)
    order = jnp.arange(plan.devs, dtype=jnp.int32) ^ lax.axis_index("dev")
    chunks = []
    for chunk in pieces:
        x = jnp.take(jnp.stack(chunk), order, axis=0)
        x = [jnp.concatenate(unfolded(x[d, at], plan), 0) for d in range(plan.devs) for at in range(3)]
        x = jnp.stack(x).reshape(plan.devs, 3, plan.rows, plan.chunk_width)
        chunks.append(x.transpose(1, 2, 0, 3))
    out = jnp.concatenate(chunks, axis=3).reshape(3, plan.rows, plan.width)
    return out[0], out[1], out[2]


def exchange(plan, pieces):
    got = [pieces[0]] + [None] * (plan.devs - 1)
    for step in range(plan.devs - 1, 0, -1):
        pairs = [(i, i ^ step) for i in range(plan.devs)]
        got[step] = lax.ppermute(pieces[step], "dev", pairs)
    return got


def dot(a, b, over):
    return lax.dot_general(a, b, ((over[:1], over[1:]), ((), ())), preferred_element_type=F32)


def of_head(x, head, plan):
    if plan.heads == 1:
        return x
    lane = lax.broadcasted_iota(jnp.int32, x.shape, 1)
    own = (lane >= head * plan.dim) & (lane < (head + 1) * plan.dim)
    return jnp.where(own, x, jnp.zeros_like(x))


def joined(parts, plan):
    columns = []
    for first in range(0, plan.chunk_width, 128):
        end = min(first + 128, plan.chunk_width)
        out = None
        for head in range(plan.heads):
            if head * plan.dim >= end or (head + 1) * plan.dim <= first:
                continue
            x = parts[head][:, first:end]
            if out is None:
                out = x
            else:
                lane = first + lax.broadcasted_iota(jnp.int32, x.shape, 1)
                out = jnp.where(lane < head * plan.dim, out, x)
        columns.append(out)
    return columns[0] if len(columns) == 1 else jnp.concatenate(columns, axis=1)


def block_parts(first, plan):
    for part in range(plan.fold):
        start = first + part * plan.fold_rows
        yield part, pl.ds(pl.multiple_of(start, plan.fold_rows), plan.fold_rows)


def teacher_rows(plan, q, k, v):
    parts = []
    for head in range(plan.heads):
        scores = dot(of_head(q, head, plan), k, (1, 1))
        top = scores.max(-1, keepdims=True)
        e = jnp.exp2((scores - top) * (plan.scale * LOG2E))
        parts.append(dot(e.astype(BF16), v, (1, 0)) * (1.0 / e.sum(-1, keepdims=True)))
    return joined(parts, plan).astype(BF16)


def student_group(plan, q, k, v, target, open_far):
    rows, reach, heads = plan.rows, plan.reach, range(plan.heads)
    at_query = lax.broadcasted_iota(jnp.int32, (rows, rows), 0)
    at_key = lax.broadcasted_iota(jnp.int32, (rows, rows), 1)
    late, early = at_key >= at_query, at_key <= at_query

    def seen(i, block, j):
        mask = None
        if j == i:
            mask = late
        elif j == i + reach:
            mask = early
        if open_far is not None and j < reach:
            mask = jnp.broadcast_to(open_far, (rows, rows)) if mask is None else mask & open_far
        return block if mask is None else jnp.where(mask, block, NEGATIVE)

    def window(x, i):
        return x[i * rows : (i + 1) * rows, i * rows : (i + reach + 1) * rows]

    def whole(parts):
        lines = []
        for i, x in enumerate(parts):
            left = [jnp.zeros((rows, i * rows), x.dtype)] if i else []
            right = [jnp.zeros((rows, (reach - 1 - i) * rows), x.dtype)] if i < reach - 1 else []
            lines.append(jnp.concatenate(left + [x] + right, axis=1))
        return lines[0] if reach == 1 else jnp.concatenate(lines, axis=0)

    weights, probability, outs = [], [], []
    for head in heads:
        scores = dot(of_head(q, head, plan), k, (1, 1))
        ps = []
        for i in range(reach):
            s = window(scores, i)
            s = [seen(i, s[:, j * rows : (j + 1) * rows], i + j) for j in range(reach + 1)]
            s = jnp.concatenate(s, axis=1)
            top = s.max(-1, keepdims=True)
            e = jnp.exp2((s - top) * (plan.scale * LOG2E))
            ps.append(e * (1.0 / e.sum(-1, keepdims=True)))
        probability.append(ps)
        weights.append(whole([p.astype(BF16) for p in ps]))
        outs.append(dot(weights[head], v, (1, 0)))
    d_out = (128.0 * (joined(outs, plan) - target.astype(F32))).astype(BF16)
    gq, gk, gv = [], [], []
    for head in heads:
        d_prob = dot(of_head(d_out, head, plan), v, (1, 1))
        ds = []
        for i, p in enumerate(probability[head]):
            d = window(d_prob, i)
            inner = (p * d).sum(-1, keepdims=True)
            ds.append((p * (d - inner) * plan.scale).astype(BF16))
        d_scores = whole(ds)
        gq.append(dot(d_scores, k, (1, 0)))
        gk.append(dot(d_scores, q, (0, 0)))
        gv.append(dot(weights[head], d_out, (0, 0)))
    return joined(gq, plan), joined(gk, plan), joined(gv, plan)


def teacher_kernel(plan, *refs):
    me = lax.axis_index("dev")
    piece_refs, (q_ref, k_ref, v_ref, target_ref) = refs[: plan.devs], refs[plan.devs :]
    for step, ref in enumerate(piece_refs):
        for at, to in enumerate((q_ref, k_ref, v_ref)):
            groups = unfolded(ref[at], plan)
            for part, rows in block_parts((me ^ step) * plan.rows, plan):
                to[rows, :] = groups[part]
    count = plan.teacher_rows
    if count == plan.seg_rows:
        target_ref[...] = teacher_rows(plan, q_ref[...], k_ref[...], v_ref[...])
        return

    def body(i, _):
        rows = pl.ds(pl.multiple_of(i * count, count), count)
        target_ref[rows, :] = teacher_rows(plan, q_ref[rows, :], k_ref[...], v_ref[...])
        return 0

    lax.fori_loop(0, plan.seg_rows // count, body, 0)


def teacher(plan, pieces):
    outs = [shape((plan.seg_rows, plan.chunk_width))] * 4
    flops = 4 * plan.heads * plan.seg_rows * plan.seg_rows * plan.dim
    return call(functools.partial(teacher_kernel, plan), list(pieces), outs, (), flops)


def first_kernel(plan, q_ref, k_ref, v_ref, target_ref, halo_ref, gq_ref, gk_ref, gv_ref, far_ref, ext):
    near = plan.near
    for at, ref in enumerate((k_ref, v_ref)):
        for block in range(plan.reach):
            groups = unfolded(halo_ref[block, at], plan)
            for part, rows in block_parts(block * plan.rows, plan):
                ext[at, rows, :] = groups[part]
        ext[at, near:, :] = ref[:near, :]
    open_far = lax.axis_index("seg") > 0
    gq, gk, gv = student_group(plan, q_ref[:near, :], ext[0], ext[1], target_ref[:near, :], open_far)
    gq_ref[...] = gq.astype(BF16)
    for at, (grad, ref) in enumerate(((gk, gk_ref), (gv, gv_ref))):
        ref[...] = grad[near:]
        for block in range(plan.reach):
            rows = slice(block * plan.rows, (block + 1) * plan.rows)
            far_ref[block, at] = folded(grad[rows].astype(BF16), plan)


def first_group(plan, held, halo):
    near, width = plan.near, plan.chunk_width
    outs = [
        shape((near, width)),
        shape((near, width), F32),
        shape((near, width), F32),
        shape((plan.reach, 2) + plan.piece),
    ]
    scratch = [pltpu.VMEM((2, 2 * near, width), BF16)]
    flops = 24 * plan.heads * near * near * plan.dim
    return call(functools.partial(first_kernel, plan), list(held) + [halo], outs, scratch, flops)


def rest_kernel(plan, q_ref, k_ref, v_ref, target_ref, k_start, v_start, gq_ref, gk_ref, gv_ref):
    near = plan.near

    def group(start):
        rows, keys = pl.ds(start + near, near), pl.ds(start, 2 * near)
        args = (q_ref[rows, :], k_ref[keys, :], v_ref[keys, :], target_ref[rows, :])
        return student_group(plan, *args, None)

    if plan.groups == 2:
        gq, gk, gv = group(0)
        gq_ref[...] = gq.astype(BF16)
        for grad, start, ref in ((gk, k_start, gk_ref), (gv, v_start, gv_ref)):
            ref[:near, :] = grad[:near] + start[...]
            ref[near:, :] = grad[near:]
        return
    for start, ref in ((k_start, gk_ref), (v_start, gv_ref)):
        ref[:near, :] = start[...]
        ref[near:, :] = jnp.zeros((plan.seg_rows - near, plan.chunk_width), F32)

    def body(i, _):
        start = pl.multiple_of(i * near, near)
        gq, gk, gv = group(start)
        gq_ref[pl.ds(start, near), :] = gq.astype(BF16)
        gk_ref[pl.ds(start, 2 * near), :] += gk
        gv_ref[pl.ds(start, 2 * near), :] += gv
        return 0

    lax.fori_loop(0, plan.groups - 1, body, 0)


def rest_groups(plan, held, starts):
    near, width = plan.near, plan.chunk_width
    count = plan.seg_rows - near
    outs = [
        shape((count, width)),
        shape((plan.seg_rows, width), F32),
        shape((plan.seg_rows, width), F32),
    ]
    flops = 24 * plan.heads * count * near * plan.dim
    return call(functools.partial(rest_kernel, plan), list(held) + list(starts), outs, (), flops)


def finish_kernel(plan, gq_first, gq_rest, gk, gv, far, *refs):
    me = lax.axis_index("dev")
    out_refs, (grads,) = refs[: plan.devs], refs[plan.devs :]
    near = plan.near
    last = plan.seg_rows - near
    grads[0, :near, :] = gq_first[...]
    grads[0, near:, :] = gq_rest[...]
    for at, ref in enumerate((gk, gv)):
        grads[1 + at, :last, :] = ref[:last, :].astype(BF16)
        for block in range(plan.reach):
            groups = unfolded(far[block, at], plan)
            for part, rows in block_parts(last + block * plan.rows, plan):
                grads[1 + at, rows, :] = (ref[rows, :] + groups[part].astype(F32)).astype(BF16)
    for step, out_ref in enumerate(out_refs):
        rows = pl.ds(pl.multiple_of((me ^ step) * plan.rows, plan.rows), plan.rows)
        for at in range(3):
            out_ref[at] = folded(grads[at, rows, :], plan)


def finish(plan, gq_first, gq_rest, gk, gv, far):
    outs = [shape((3,) + plan.piece) for _ in range(plan.devs)]
    scratch = [pltpu.VMEM((3, plan.seg_rows, plan.chunk_width), BF16)]
    arrays = [gq_first, gq_rest, gk, gv, far]
    return call(functools.partial(finish_kernel, plan), arrays, outs, scratch)


def local(queries, keys, values):
    rows, width = queries.shape
    plan = Plan(rows, width, lax.axis_size("dev"))
    seg_count = lax.axis_size("seg")
    onward = [(i, i + 1) for i in range(seg_count - 1)]
    backward = [(i + 1, i) for i in range(seg_count - 1)]
    me = lax.axis_index("dev")
    packed = pack(plan, [queries, keys, values])
    arrived = []
    for pieces in packed:
        arrived.append(exchange(plan, pieces))
    returned = []
    for pieces in arrived:
        halo = jnp.stack(
            [
                lax.select_n((plan.devs - plan.reach + b) ^ me, *[p[1:] for p in pieces])
                for b in range(plan.reach)
            ]
        )
        halo = lax.ppermute(halo, "seg", onward)
        held = teacher(plan, pieces)
        gq_first, gk, gv, far = first_group(plan, held, halo)
        far = lax.ppermute(far, "seg", backward)
        gq_rest, gk, gv = rest_groups(plan, held, (gk, gv))
        pieces = finish(plan, gq_first, gq_rest, gk, gv, far)
        returned.append(exchange(plan, pieces))
    return tuple(unpack(plan, returned))


def solution(mesh):
    spec = P(("seg", "dev"), None)
    return jax.shard_map(
        local, mesh=mesh, in_specs=(spec,) * 3, out_specs=(spec,) * 3, check_vma=False
    )
```

```python
import functools
import math

import jax
import jax.numpy as jnp
from jax import lax
from jax.experimental import pallas as pl
from jax.experimental.pallas import tpu as pltpu
from jax.sharding import PartitionSpec as P


HEADS = 16
WINDOW = 256
CHUNKS = 2
PACK_MIB = 58
NEGATIVE = -1e30
LOG2E = math.log2(math.e)
BF16 = jnp.bfloat16
F32 = jnp.float32


VMEM_SPEC = pl.BlockSpec(memory_space=pltpu.VMEM)
HBM_SPEC = pl.BlockSpec(memory_space=pltpu.HBM)


def call(kernel, arrays, outs, scratch=(), flops=0, spec=VMEM_SPEC, out_spec=VMEM_SPEC, vmem=48):
    moved = sum(a.size * a.dtype.itemsize for a in arrays)
    moved += sum(math.prod(o.shape) * o.dtype.itemsize for o in outs)
    return pl.pallas_call(
        kernel,
        out_shape=tuple(outs),
        in_specs=[spec] * len(arrays),
        out_specs=tuple([out_spec] * len(outs)),
        scratch_shapes=list(scratch),
        cost_estimate=pl.CostEstimate(flops=flops, bytes_accessed=moved, transcendentals=0),
        compiler_params=pltpu.CompilerParams(vmem_limit_bytes=vmem * 1024 * 1024),
    )(*arrays)


def shape(dims, dtype=BF16):
    return jax.ShapeDtypeStruct(dims, dtype)


class Plan:
    def __init__(self, rows, width, devs):
        self.rows, self.width, self.devs = rows, width, devs
        self.dim = width // HEADS
        self.local_heads = HEADS // devs
        self.local_width = width // devs
        self.chunks = CHUNKS if self.local_heads % CHUNKS == 0 else 1
        self.heads = self.local_heads // self.chunks
        self.chunk_width = self.heads * self.dim
        self.fold = 128 // math.gcd(self.chunk_width, 128)
        self.fold_rows = rows // self.fold
        self.piece = (self.fold_rows, self.fold * self.chunk_width)
        self.reach = WINDOW // rows
        self.seg_rows = rows * devs
        self.near = self.reach * rows
        self.groups = self.seg_rows // self.near
        self.teacher_rows = self.seg_rows if self.seg_rows <= 512 else rows
        self.scale = self.dim ** (-0.5)


def folded(x, plan):
    full = plan.chunk_width // 128 * 128
    parts = [x[i * plan.fold_rows : (i + 1) * plan.fold_rows] for i in range(plan.fold)]
    columns = [p[:, at : at + 128] for at in range(0, full, 128) for p in parts]
    if plan.chunk_width > full:
        columns += [p[:, full:] for p in parts]
    return columns[0] if len(columns) == 1 else jnp.concatenate(columns, axis=1)


def unfolded(x, plan):
    full = plan.chunk_width // 128 * 128
    rest = plan.chunk_width - full
    groups = []
    for i in range(plan.fold):
        columns = [
            x[:, at * plan.fold + i * 128 : at * plan.fold + (i + 1) * 128]
            for at in range(0, full, 128)
        ]
        if rest:
            start = plan.fold * full + i * rest
            columns.append(x[:, start : start + rest])
        groups.append(columns[0] if len(columns) == 1 else jnp.concatenate(columns, axis=1))
    return groups


def columns_of(x, chunk, plan):
    return folded(x[:, chunk * plan.chunk_width : (chunk + 1) * plan.chunk_width], plan)


def pack_first_kernel(plan, *refs):
    me = lax.axis_index("dev")
    in_refs, out_refs, (held, made, in_sems, out_sems) = refs[:3], refs[3:-4], refs[-4:]
    steps = range(plan.devs - 1, 0, -1)

    def taken(step, at):
        start = pl.multiple_of((me ^ step) * plan.local_width, 128)
        block = in_refs[at].at[:, pl.ds(start, plan.local_width)]
        return pltpu.make_async_copy(block, held.at[step - 1, at], in_sems.at[step - 1, at])

    def given(step):
        return pltpu.make_async_copy(
            made.at[step - 1], out_refs[step - 1], out_sems.at[step - 1]
        )

    for step in steps:
        for at in range(3):
            taken(step, at).start()
    for step in steps:
        for at in range(3):
            taken(step, at).wait()
            made[step - 1, at] = columns_of(held[step - 1, at], 0, plan)
        given(step).start()
    for step in steps:
        given(step).wait()


def pack_rest_kernel(plan, chunk, *refs):
    me = lax.axis_index("dev")
    in_refs, out_refs = refs[:3], refs[3:]
    for at in range(3):
        for step in range(plan.devs):
            start = pl.multiple_of((me ^ step) * plan.local_width, 128)
            x = in_refs[at][:, pl.ds(start, plan.local_width)]
            out_refs[step][at] = columns_of(x, chunk, plan)
            if chunk == 1 and step == 0:
                out_refs[plan.devs][at] = columns_of(x, 0, plan)


def pack(plan, arrays):
    piece = shape((3,) + plan.piece)
    chunks = []
    if plan.local_width % 128 == 0 and plan.chunks > 1:
        others = plan.devs - 1
        scratch = [
            pltpu.VMEM((others, 3, plan.rows, plan.local_width), BF16),
            pltpu.VMEM((others, 3) + plan.piece, BF16),
            pltpu.SemaphoreType.DMA((others, 3)),
            pltpu.SemaphoreType.DMA((others,)),
        ]
        kernel = functools.partial(pack_first_kernel, plan)
        sent = call(
            kernel, arrays, [piece] * others, scratch, spec=HBM_SPEC, out_spec=HBM_SPEC, vmem=PACK_MIB
        )
        chunks.append([None] + list(sent))
        for chunk in range(1, plan.chunks):
            kernel = functools.partial(pack_rest_kernel, plan, chunk)
            got = list(call(kernel, arrays, [piece] * (plan.devs + (chunk == 1))))
            if chunk == 1:
                chunks[0][0] = got.pop()
            chunks.append(got)
        return chunks
    me = lax.axis_index("dev")
    for chunk in range(plan.chunks):
        pieces = []
        for step in range(plan.devs):
            start = (me ^ step) * plan.local_width + chunk * plan.chunk_width
            taken = [lax.dynamic_slice_in_dim(a, start, plan.chunk_width, 1) for a in arrays]
            pieces.append(jnp.stack([folded(x, plan) for x in taken]))
        chunks.append(pieces)
    return chunks


def unpack_kernel(plan, *refs):
    me = lax.axis_index("dev")
    piece_refs, out_refs, (held, sems) = refs[:-5], refs[-5:-2], refs[-2:]

    def given(step, at):
        start = pl.multiple_of((me ^ step) * plan.local_width, 128)
        block = out_refs[at].at[:, pl.ds(start, plan.local_width)]
        return pltpu.make_async_copy(held.at[step, at], block, sems.at[step, at])

    for step in range(plan.devs):
        for at in range(3):
            got = [unfolded(piece_refs[c * plan.devs + step][at], plan) for c in range(plan.chunks)]
            for part in range(plan.fold):
                rows = slice(part * plan.fold_rows, (part + 1) * plan.fold_rows)
                x = [groups[part] for groups in got]
                held[step, at, rows, :] = x[0] if plan.chunks == 1 else jnp.concatenate(x, axis=1)
            given(step, at).start()
    for step in range(plan.devs):
        for at in range(3):
            given(step, at).wait()


def unpack(plan, pieces):
    if plan.local_width % 128 == 0:
        flat = [piece for chunk in pieces for piece in chunk]
        outs = [shape((plan.rows, plan.width)) for _ in range(3)]
        scratch = [
            pltpu.VMEM((plan.devs, 3, plan.rows, plan.local_width), BF16),
            pltpu.SemaphoreType.DMA((plan.devs, 3)),
        ]
        kernel = functools.partial(unpack_kernel, plan)
        return call(kernel, flat, outs, scratch, out_spec=HBM_SPEC)
    order = jnp.arange(plan.devs, dtype=jnp.int32) ^ lax.axis_index("dev")
    chunks = []
    for chunk in pieces:
        x = jnp.take(jnp.stack(chunk), order, axis=0)
        x = [jnp.concatenate(unfolded(x[d, at], plan), 0) for d in range(plan.devs) for at in range(3)]
        x = jnp.stack(x).reshape(plan.devs, 3, plan.rows, plan.chunk_width)
        chunks.append(x.transpose(1, 2, 0, 3))
    out = jnp.concatenate(chunks, axis=3).reshape(3, plan.rows, plan.width)
    return out[0], out[1], out[2]


def exchange(plan, pieces):
    got = [pieces[0]] + [None] * (plan.devs - 1)
    for step in range(plan.devs - 1, 0, -1):
        pairs = [(i, i ^ step) for i in range(plan.devs)]
        got[step] = lax.ppermute(pieces[step], "dev", pairs)
    return got


def dot(a, b, over):
    return lax.dot_general(a, b, ((over[:1], over[1:]), ((), ())), preferred_element_type=F32)


def dot_heads(parts, b, over):
    axis = 1 - over[0]
    count = parts[0].shape[axis]
    out = dot(jnp.concatenate(parts, axis=axis), b, over)
    return [out[i * count : (i + 1) * count] for i in range(len(parts))]


def of_head(x, head, plan):
    if plan.heads == 1:
        return x
    lane = lax.broadcasted_iota(jnp.int32, x.shape, 1)
    own = (lane >= head * plan.dim) & (lane < (head + 1) * plan.dim)
    return jnp.where(own, x, jnp.zeros_like(x))


def joined(parts, plan):
    columns = []
    for first in range(0, plan.chunk_width, 128):
        end = min(first + 128, plan.chunk_width)
        out = None
        for head in range(plan.heads):
            if head * plan.dim >= end or (head + 1) * plan.dim <= first:
                continue
            x = parts[head][:, first:end]
            if out is None:
                out = x
            else:
                lane = first + lax.broadcasted_iota(jnp.int32, x.shape, 1)
                out = jnp.where(lane < head * plan.dim, out, x)
        columns.append(out)
    return columns[0] if len(columns) == 1 else jnp.concatenate(columns, axis=1)


def block_parts(first, plan):
    for part in range(plan.fold):
        start = first + part * plan.fold_rows
        yield part, pl.ds(pl.multiple_of(start, plan.fold_rows), plan.fold_rows)


def teacher_rows(plan, q, k, v):
    parts = []
    scores = [dot(of_head(q, head, plan), k, (1, 1)) for head in range(plan.heads)]
    for s in scores:
        e = jnp.exp2((s - s.max(-1, keepdims=True)) * (plan.scale * LOG2E))
        parts.append(dot(e.astype(BF16), v, (1, 0)) * (1.0 / e.sum(-1, keepdims=True)))
    return joined(parts, plan).astype(BF16)


def student_group(plan, q, k, v, target, open_far):
    rows, reach, heads = plan.rows, plan.reach, range(plan.heads)
    at_query = lax.broadcasted_iota(jnp.int32, (rows, rows), 0)
    at_key = lax.broadcasted_iota(jnp.int32, (rows, rows), 1)
    late, early = at_key >= at_query, at_key <= at_query

    def seen(i, block, j):
        mask = None
        if j == i:
            mask = late
        elif j == i + reach:
            mask = early
        if open_far is not None and j < reach:
            mask = jnp.broadcast_to(open_far, (rows, rows)) if mask is None else mask & open_far
        return block if mask is None else jnp.where(mask, block, NEGATIVE)

    def window(x, i):
        return x[i * rows : (i + 1) * rows, i * rows : (i + reach + 1) * rows]

    def whole(parts):
        lines = []
        for i, x in enumerate(parts):
            left = [jnp.zeros((rows, i * rows), x.dtype)] if i else []
            right = [jnp.zeros((rows, (reach - 1 - i) * rows), x.dtype)] if i < reach - 1 else []
            lines.append(jnp.concatenate(left + [x] + right, axis=1))
        return lines[0] if reach == 1 else jnp.concatenate(lines, axis=0)

    scores = [dot(of_head(q, head, plan), k, (1, 1)) for head in heads]
    weights, probability, outs = [], [], []
    for head in heads:
        ps = []
        for i in range(reach):
            s = window(scores[head], i)
            s = [seen(i, s[:, j * rows : (j + 1) * rows], i + j) for j in range(reach + 1)]
            s = jnp.concatenate(s, axis=1)
            top = s.max(-1, keepdims=True)
            e = jnp.exp2((s - top) * (plan.scale * LOG2E))
            ps.append(e * (1.0 / e.sum(-1, keepdims=True)))
        probability.append(ps)
        weights.append(whole([p.astype(BF16) for p in ps]))
        outs.append(dot(weights[head], v, (1, 0)))
    d_out = (128.0 * (joined(outs, plan) - target.astype(F32))).astype(BF16)
    d_prob = [dot(of_head(d_out, head, plan), v, (1, 1)) for head in heads]
    gv = dot_heads(weights, d_out, (0, 0))
    d_scores = []
    for head in heads:
        ds = []
        for i, p in enumerate(probability[head]):
            d = window(d_prob[head], i)
            inner = (p * d).sum(-1, keepdims=True)
            ds.append((p * (d - inner) * plan.scale).astype(BF16))
        d_scores.append(whole(ds))
    gk = dot_heads(d_scores, q, (0, 0))
    gq = dot_heads(d_scores, k, (1, 0))
    return joined(gq, plan), joined(gk, plan), joined(gv, plan)


def teacher_kernel(plan, *refs):
    me = lax.axis_index("dev")
    piece_refs, (q_ref, k_ref, v_ref, target_ref) = refs[: plan.devs], refs[plan.devs :]
    for step, ref in enumerate(piece_refs):
        for at, to in enumerate((q_ref, k_ref, v_ref)):
            groups = unfolded(ref[at], plan)
            for part, rows in block_parts((me ^ step) * plan.rows, plan):
                to[rows, :] = groups[part]
    count = plan.teacher_rows
    if count == plan.seg_rows:
        target_ref[...] = teacher_rows(plan, q_ref[...], k_ref[...], v_ref[...])
        return

    def body(i, _):
        rows = pl.ds(pl.multiple_of(i * count, count), count)
        target_ref[rows, :] = teacher_rows(plan, q_ref[rows, :], k_ref[...], v_ref[...])
        return 0

    lax.fori_loop(0, plan.seg_rows // count, body, 0)


def teacher(plan, pieces):
    outs = [shape((plan.seg_rows, plan.chunk_width))] * 4
    flops = 4 * plan.heads * plan.seg_rows * plan.seg_rows * plan.dim
    return call(functools.partial(teacher_kernel, plan), list(pieces), outs, (), flops)


def first_kernel(plan, q_ref, k_ref, v_ref, target_ref, halo_ref, gq_ref, gk_ref, gv_ref, far_ref, ext):
    near = plan.near
    for at, ref in enumerate((k_ref, v_ref)):
        for block in range(plan.reach):
            groups = unfolded(halo_ref[block, at], plan)
            for part, rows in block_parts(block * plan.rows, plan):
                ext[at, rows, :] = groups[part]
        ext[at, near:, :] = ref[:near, :]
    open_far = lax.axis_index("seg") > 0
    gq, gk, gv = student_group(plan, q_ref[:near, :], ext[0], ext[1], target_ref[:near, :], open_far)
    gq_ref[...] = gq.astype(BF16)
    for at, (grad, ref) in enumerate(((gk, gk_ref), (gv, gv_ref))):
        ref[...] = grad[near:]
        for block in range(plan.reach):
            rows = slice(block * plan.rows, (block + 1) * plan.rows)
            far_ref[block, at] = folded(grad[rows].astype(BF16), plan)


def first_group(plan, held, halo):
    near, width = plan.near, plan.chunk_width
    outs = [
        shape((near, width)),
        shape((near, width), F32),
        shape((near, width), F32),
        shape((plan.reach, 2) + plan.piece),
    ]
    scratch = [pltpu.VMEM((2, 2 * near, width), BF16)]
    flops = 24 * plan.heads * near * near * plan.dim
    return call(functools.partial(first_kernel, plan), list(held) + [halo], outs, scratch, flops)


def rest_kernel(plan, q_ref, k_ref, v_ref, target_ref, k_start, v_start, gq_ref, gk_ref, gv_ref):
    near = plan.near

    def group(start):
        rows, keys = pl.ds(start + near, near), pl.ds(start, 2 * near)
        args = (q_ref[rows, :], k_ref[keys, :], v_ref[keys, :], target_ref[rows, :])
        return student_group(plan, *args, None)

    if plan.groups == 2:
        gq, gk, gv = group(0)
        gq_ref[...] = gq.astype(BF16)
        for grad, start, ref in ((gk, k_start, gk_ref), (gv, v_start, gv_ref)):
            ref[:near, :] = grad[:near] + start[...]
            ref[near:, :] = grad[near:]
        return
    for start, ref in ((k_start, gk_ref), (v_start, gv_ref)):
        ref[:near, :] = start[...]
        ref[near:, :] = jnp.zeros((plan.seg_rows - near, plan.chunk_width), F32)

    def body(i, _):
        start = pl.multiple_of(i * near, near)
        gq, gk, gv = group(start)
        gq_ref[pl.ds(start, near), :] = gq.astype(BF16)
        gk_ref[pl.ds(start, 2 * near), :] += gk
        gv_ref[pl.ds(start, 2 * near), :] += gv
        return 0

    lax.fori_loop(0, plan.groups - 1, body, 0)


def rest_groups(plan, held, starts):
    near, width = plan.near, plan.chunk_width
    count = plan.seg_rows - near
    outs = [
        shape((count, width)),
        shape((plan.seg_rows, width), F32),
        shape((plan.seg_rows, width), F32),
    ]
    flops = 24 * plan.heads * count * near * plan.dim
    return call(functools.partial(rest_kernel, plan), list(held) + list(starts), outs, (), flops)


def finish_kernel(plan, gq_first, gq_rest, gk, gv, far, *refs):
    me = lax.axis_index("dev")
    out_refs, (grads,) = refs[: plan.devs], refs[plan.devs :]
    near = plan.near
    last = plan.seg_rows - near
    grads[0, :near, :] = gq_first[...]
    grads[0, near:, :] = gq_rest[...]
    for at, ref in enumerate((gk, gv)):
        grads[1 + at, :last, :] = ref[:last, :].astype(BF16)
        for block in range(plan.reach):
            groups = unfolded(far[block, at], plan)
            for part, rows in block_parts(last + block * plan.rows, plan):
                grads[1 + at, rows, :] = (ref[rows, :] + groups[part].astype(F32)).astype(BF16)
    for step, out_ref in enumerate(out_refs):
        rows = pl.ds(pl.multiple_of((me ^ step) * plan.rows, plan.rows), plan.rows)
        for at in range(3):
            out_ref[at] = folded(grads[at, rows, :], plan)


def finish(plan, gq_first, gq_rest, gk, gv, far):
    outs = [shape((3,) + plan.piece) for _ in range(plan.devs)]
    scratch = [pltpu.VMEM((3, plan.seg_rows, plan.chunk_width), BF16)]
    arrays = [gq_first, gq_rest, gk, gv, far]
    return call(functools.partial(finish_kernel, plan), arrays, outs, scratch)


def local(queries, keys, values):
    rows, width = queries.shape
    plan = Plan(rows, width, lax.axis_size("dev"))
    seg_count = lax.axis_size("seg")
    onward = [(i, i + 1) for i in range(seg_count - 1)]
    backward = [(i + 1, i) for i in range(seg_count - 1)]
    me = lax.axis_index("dev")
    packed = pack(plan, [queries, keys, values])
    arrived = []
    for pieces in packed:
        arrived.append(exchange(plan, pieces))
    returned = []
    for pieces in arrived:
        halo = jnp.stack(
            [
                lax.select_n((plan.devs - plan.reach + b) ^ me, *[p[1:] for p in pieces])
                for b in range(plan.reach)
            ]
        )
        halo = lax.ppermute(halo, "seg", onward)
        held = teacher(plan, pieces)
        gq_first, gk, gv, far = first_group(plan, held, halo)
        far = lax.ppermute(far, "seg", backward)
        gq_rest, gk, gv = rest_groups(plan, held, (gk, gv))
        pieces = finish(plan, gq_first, gq_rest, gk, gv, far)
        returned.append(exchange(plan, pieces))
    return tuple(unpack(plan, returned))


def solution(mesh):
    spec = P(("seg", "dev"), None)
    return jax.shard_map(
        local, mesh=mesh, in_specs=(spec,) * 3, out_specs=(spec,) * 3, check_vma=False
    )
```

```python
import functools
import math

import jax
import jax.numpy as jnp
from jax import lax
from jax.experimental import pallas as pl
from jax.experimental.pallas import tpu as pltpu
from jax.sharding import PartitionSpec as P


HEADS = 16
WINDOW = 256
CHUNKS = 2
NEGATIVE = -1e30
LOG2E = math.log2(math.e)
BF16 = jnp.bfloat16
F32 = jnp.float32


VMEM_SPEC = pl.BlockSpec(memory_space=pltpu.VMEM)
HBM_SPEC = pl.BlockSpec(memory_space=pltpu.HBM)


def call(kernel, arrays, outs, scratch=(), flops=0, spec=VMEM_SPEC, out_spec=VMEM_SPEC):
    moved = sum(a.size * a.dtype.itemsize for a in arrays)
    moved += sum(math.prod(o.shape) * o.dtype.itemsize for o in outs)
    return pl.pallas_call(
        kernel,
        out_shape=tuple(outs),
        in_specs=[spec] * len(arrays),
        out_specs=tuple([out_spec] * len(outs)),
        scratch_shapes=list(scratch),
        cost_estimate=pl.CostEstimate(flops=flops, bytes_accessed=moved, transcendentals=0),
        compiler_params=pltpu.CompilerParams(vmem_limit_bytes=48 * 1024 * 1024),
    )(*arrays)


def shape(dims, dtype=BF16):
    return jax.ShapeDtypeStruct(dims, dtype)


class Plan:
    def __init__(self, rows, width, devs):
        self.rows, self.width, self.devs = rows, width, devs
        self.dim = width // HEADS
        self.local_heads = HEADS // devs
        self.local_width = width // devs
        self.chunks = CHUNKS if self.local_heads % CHUNKS == 0 else 1
        self.heads = self.local_heads // self.chunks
        self.chunk_width = self.heads * self.dim
        self.fold = 128 // math.gcd(self.chunk_width, 128)
        self.fold_rows = rows // self.fold
        self.piece = (self.fold_rows, self.fold * self.chunk_width)
        self.reach = WINDOW // rows
        self.seg_rows = rows * devs
        self.near = self.reach * rows
        self.groups = self.seg_rows // self.near
        self.teacher_rows = self.seg_rows if self.seg_rows <= 512 else rows
        self.scale = self.dim ** (-0.5)


def folded(x, plan):
    full = plan.chunk_width // 128 * 128
    parts = [x[i * plan.fold_rows : (i + 1) * plan.fold_rows] for i in range(plan.fold)]
    columns = [p[:, at : at + 128] for at in range(0, full, 128) for p in parts]
    if plan.chunk_width > full:
        columns += [p[:, full:] for p in parts]
    return columns[0] if len(columns) == 1 else jnp.concatenate(columns, axis=1)


def unfolded(x, plan):
    full = plan.chunk_width // 128 * 128
    rest = plan.chunk_width - full
    groups = []
    for i in range(plan.fold):
        columns = [
            x[:, at * plan.fold + i * 128 : at * plan.fold + (i + 1) * 128]
            for at in range(0, full, 128)
        ]
        if rest:
            start = plan.fold * full + i * rest
            columns.append(x[:, start : start + rest])
        groups.append(columns[0] if len(columns) == 1 else jnp.concatenate(columns, axis=1))
    return groups


def columns_of(x, chunk, plan):
    return folded(x[:, chunk * plan.chunk_width : (chunk + 1) * plan.chunk_width], plan)


def pack_first_kernel(plan, steps, *refs):
    me = lax.axis_index("dev")
    in_refs, out_refs, (held, sems) = refs[:3], refs[3:-2], refs[-2:]

    def taken(i, at):
        start = pl.multiple_of((me ^ steps[i]) * plan.local_width, 128)
        block = in_refs[at].at[:, pl.ds(start, plan.local_width)]
        return pltpu.make_async_copy(block, held.at[i, at], sems.at[i, at])

    each = [(i, at) for i in range(len(steps)) for at in range(3)]
    for i, at in each:
        taken(i, at).start()
    for i, at in each:
        taken(i, at).wait()
        out_refs[i][at] = columns_of(held[i, at], 0, plan)


def pack_rest_kernel(plan, chunk, *refs):
    me = lax.axis_index("dev")
    in_refs, out_refs = refs[:3], refs[3:]
    for at in range(3):
        for step in range(plan.devs):
            start = pl.multiple_of((me ^ step) * plan.local_width, 128)
            x = in_refs[at][:, pl.ds(start, plan.local_width)]
            out_refs[step][at] = columns_of(x, chunk, plan)
            if chunk == 1 and step == 0:
                out_refs[plan.devs][at] = columns_of(x, 0, plan)


def pack(plan, arrays):
    piece = shape((3,) + plan.piece)
    chunks = []
    if plan.local_width % 128 == 0 and plan.chunks > 1:
        sent = [None] * plan.devs
        far_away = plan.devs - 1
        held = [pltpu.with_memory_space_constraint(a, pltpu.HBM) for a in arrays]
        for steps in ([far_away], list(range(far_away - 1, 0, -1))):
            scratch = [
                pltpu.VMEM((len(steps), 3, plan.rows, plan.local_width), BF16),
                pltpu.SemaphoreType.DMA((len(steps), 3)),
            ]
            kernel = functools.partial(pack_first_kernel, plan, steps)
            got = call(kernel, held, [piece] * len(steps), scratch, spec=HBM_SPEC)
            for step, x in zip(steps, got):
                sent[step] = x
        chunks.append(sent)
        for chunk in range(1, plan.chunks):
            kernel = functools.partial(pack_rest_kernel, plan, chunk)
            got = list(call(kernel, arrays, [piece] * (plan.devs + (chunk == 1))))
            if chunk == 1:
                chunks[0][0] = got.pop()
            chunks.append(got)
        return chunks
    me = lax.axis_index("dev")
    for chunk in range(plan.chunks):
        pieces = []
        for step in range(plan.devs):
            start = (me ^ step) * plan.local_width + chunk * plan.chunk_width
            taken = [lax.dynamic_slice_in_dim(a, start, plan.chunk_width, 1) for a in arrays]
            pieces.append(jnp.stack([folded(x, plan) for x in taken]))
        chunks.append(pieces)
    return chunks


def unpack_kernel(plan, *refs):
    me = lax.axis_index("dev")
    piece_refs, out_refs, (held, sems) = refs[:-5], refs[-5:-2], refs[-2:]

    def given(step, at):
        start = pl.multiple_of((me ^ step) * plan.local_width, 128)
        block = out_refs[at].at[:, pl.ds(start, plan.local_width)]
        return pltpu.make_async_copy(held.at[step, at], block, sems.at[step, at])

    for step in range(plan.devs):
        for at in range(3):
            got = [unfolded(piece_refs[c * plan.devs + step][at], plan) for c in range(plan.chunks)]
            for part in range(plan.fold):
                rows = slice(part * plan.fold_rows, (part + 1) * plan.fold_rows)
                x = [groups[part] for groups in got]
                held[step, at, rows, :] = x[0] if plan.chunks == 1 else jnp.concatenate(x, axis=1)
            given(step, at).start()
    for step in range(plan.devs):
        for at in range(3):
            given(step, at).wait()


def unpack(plan, pieces):
    if plan.local_width % 128 == 0:
        flat = [piece for chunk in pieces for piece in chunk]
        outs = [shape((plan.rows, plan.width)) for _ in range(3)]
        scratch = [
            pltpu.VMEM((plan.devs, 3, plan.rows, plan.local_width), BF16),
            pltpu.SemaphoreType.DMA((plan.devs, 3)),
        ]
        kernel = functools.partial(unpack_kernel, plan)
        return call(kernel, flat, outs, scratch, out_spec=HBM_SPEC)
    order = jnp.arange(plan.devs, dtype=jnp.int32) ^ lax.axis_index("dev")
    chunks = []
    for chunk in pieces:
        x = jnp.take(jnp.stack(chunk), order, axis=0)
        x = [jnp.concatenate(unfolded(x[d, at], plan), 0) for d in range(plan.devs) for at in range(3)]
        x = jnp.stack(x).reshape(plan.devs, 3, plan.rows, plan.chunk_width)
        chunks.append(x.transpose(1, 2, 0, 3))
    out = jnp.concatenate(chunks, axis=3).reshape(3, plan.rows, plan.width)
    return out[0], out[1], out[2]


def exchange(plan, pieces):
    got = [pieces[0]] + [None] * (plan.devs - 1)
    for step in range(plan.devs - 1, 0, -1):
        pairs = [(i, i ^ step) for i in range(plan.devs)]
        got[step] = lax.ppermute(pieces[step], "dev", pairs)
    return got


def dot(a, b, over):
    return lax.dot_general(a, b, ((over[:1], over[1:]), ((), ())), preferred_element_type=F32)


def dot_heads(parts, b, over):
    axis = 1 - over[0]
    count = parts[0].shape[axis]
    out = dot(jnp.concatenate(parts, axis=axis), b, over)
    return [out[i * count : (i + 1) * count] for i in range(len(parts))]


def of_head(x, head, plan):
    if plan.heads == 1:
        return x
    lane = lax.broadcasted_iota(jnp.int32, x.shape, 1)
    own = (lane >= head * plan.dim) & (lane < (head + 1) * plan.dim)
    return jnp.where(own, x, jnp.zeros_like(x))


def joined(parts, plan):
    columns = []
    for first in range(0, plan.chunk_width, 128):
        end = min(first + 128, plan.chunk_width)
        out = None
        for head in range(plan.heads):
            if head * plan.dim >= end or (head + 1) * plan.dim <= first:
                continue
            x = parts[head][:, first:end]
            if out is None:
                out = x
            else:
                lane = first + lax.broadcasted_iota(jnp.int32, x.shape, 1)
                out = jnp.where(lane < head * plan.dim, out, x)
        columns.append(out)
    return columns[0] if len(columns) == 1 else jnp.concatenate(columns, axis=1)


def block_parts(first, plan):
    for part in range(plan.fold):
        start = first + part * plan.fold_rows
        yield part, pl.ds(pl.multiple_of(start, plan.fold_rows), plan.fold_rows)


def teacher_rows(plan, q, k, v):
    parts = []
    scores = [dot(of_head(q, head, plan), k, (1, 1)) for head in range(plan.heads)]
    for s in scores:
        e = jnp.exp2((s - s.max(-1, keepdims=True)) * (plan.scale * LOG2E))
        parts.append(dot(e.astype(BF16), v, (1, 0)) * (1.0 / e.sum(-1, keepdims=True)))
    return joined(parts, plan).astype(BF16)


def student_group(plan, q, k, v, target, open_far):
    rows, reach, heads = plan.rows, plan.reach, range(plan.heads)
    at_query = lax.broadcasted_iota(jnp.int32, (rows, rows), 0)
    at_key = lax.broadcasted_iota(jnp.int32, (rows, rows), 1)
    late, early = at_key >= at_query, at_key <= at_query

    def seen(i, block, j):
        mask = None
        if j == i:
            mask = late
        elif j == i + reach:
            mask = early
        if open_far is not None and j < reach:
            mask = jnp.broadcast_to(open_far, (rows, rows)) if mask is None else mask & open_far
        return block if mask is None else jnp.where(mask, block, NEGATIVE)

    def window(x, i):
        return x[i * rows : (i + 1) * rows, i * rows : (i + reach + 1) * rows]

    def whole(parts):
        lines = []
        for i, x in enumerate(parts):
            left = [jnp.zeros((rows, i * rows), x.dtype)] if i else []
            right = [jnp.zeros((rows, (reach - 1 - i) * rows), x.dtype)] if i < reach - 1 else []
            lines.append(jnp.concatenate(left + [x] + right, axis=1))
        return lines[0] if reach == 1 else jnp.concatenate(lines, axis=0)

    scores = [dot(of_head(q, head, plan), k, (1, 1)) for head in heads]
    weights, probability, outs = [], [], []
    for head in heads:
        ps = []
        for i in range(reach):
            s = window(scores[head], i)
            s = [seen(i, s[:, j * rows : (j + 1) * rows], i + j) for j in range(reach + 1)]
            s = jnp.concatenate(s, axis=1)
            top = s.max(-1, keepdims=True)
            e = jnp.exp2((s - top) * (plan.scale * LOG2E))
            ps.append(e * (1.0 / e.sum(-1, keepdims=True)))
        probability.append(ps)
        weights.append(whole([p.astype(BF16) for p in ps]))
        outs.append(dot(weights[head], v, (1, 0)))
    d_out = (128.0 * (joined(outs, plan) - target.astype(F32))).astype(BF16)
    d_prob = [dot(of_head(d_out, head, plan), v, (1, 1)) for head in heads]
    gv = dot_heads(weights, d_out, (0, 0))
    d_scores = []
    for head in heads:
        ds = []
        for i, p in enumerate(probability[head]):
            d = window(d_prob[head], i)
            inner = (p * d).sum(-1, keepdims=True)
            ds.append((p * (d - inner) * plan.scale).astype(BF16))
        d_scores.append(whole(ds))
    gk = dot_heads(d_scores, q, (0, 0))
    gq = dot_heads(d_scores, k, (1, 0))
    return joined(gq, plan), joined(gk, plan), joined(gv, plan)


def teacher_kernel(plan, *refs):
    me = lax.axis_index("dev")
    piece_refs, (q_ref, k_ref, v_ref, target_ref) = refs[: plan.devs], refs[plan.devs :]
    for step, ref in enumerate(piece_refs):
        for at, to in enumerate((q_ref, k_ref, v_ref)):
            groups = unfolded(ref[at], plan)
            for part, rows in block_parts((me ^ step) * plan.rows, plan):
                to[rows, :] = groups[part]
    count = plan.teacher_rows
    if count == plan.seg_rows:
        target_ref[...] = teacher_rows(plan, q_ref[...], k_ref[...], v_ref[...])
        return

    def body(i, _):
        rows = pl.ds(pl.multiple_of(i * count, count), count)
        target_ref[rows, :] = teacher_rows(plan, q_ref[rows, :], k_ref[...], v_ref[...])
        return 0

    lax.fori_loop(0, plan.seg_rows // count, body, 0)


def teacher(plan, pieces):
    outs = [shape((plan.seg_rows, plan.chunk_width))] * 4
    flops = 4 * plan.heads * plan.seg_rows * plan.seg_rows * plan.dim
    return call(functools.partial(teacher_kernel, plan), list(pieces), outs, (), flops)


def first_kernel(plan, q_ref, k_ref, v_ref, target_ref, halo_ref, gq_ref, gk_ref, gv_ref, far_ref, ext):
    near = plan.near
    for at, ref in enumerate((k_ref, v_ref)):
        for block in range(plan.reach):
            groups = unfolded(halo_ref[block, at], plan)
            for part, rows in block_parts(block * plan.rows, plan):
                ext[at, rows, :] = groups[part]
        ext[at, near:, :] = ref[:near, :]
    open_far = lax.axis_index("seg") > 0
    gq, gk, gv = student_group(plan, q_ref[:near, :], ext[0], ext[1], target_ref[:near, :], open_far)
    gq_ref[...] = gq.astype(BF16)
    for at, (grad, ref) in enumerate(((gk, gk_ref), (gv, gv_ref))):
        ref[...] = grad[near:]
        for block in range(plan.reach):
            rows = slice(block * plan.rows, (block + 1) * plan.rows)
            far_ref[block, at] = folded(grad[rows].astype(BF16), plan)


def first_group(plan, held, halo):
    near, width = plan.near, plan.chunk_width
    outs = [
        shape((near, width)),
        shape((near, width), F32),
        shape((near, width), F32),
        shape((plan.reach, 2) + plan.piece),
    ]
    scratch = [pltpu.VMEM((2, 2 * near, width), BF16)]
    flops = 24 * plan.heads * near * near * plan.dim
    return call(functools.partial(first_kernel, plan), list(held) + [halo], outs, scratch, flops)


def rest_kernel(plan, q_ref, k_ref, v_ref, target_ref, k_start, v_start, gq_ref, gk_ref, gv_ref):
    near = plan.near

    def group(start):
        rows, keys = pl.ds(start + near, near), pl.ds(start, 2 * near)
        args = (q_ref[rows, :], k_ref[keys, :], v_ref[keys, :], target_ref[rows, :])
        return student_group(plan, *args, None)

    if plan.groups == 2:
        gq, gk, gv = group(0)
        gq_ref[...] = gq.astype(BF16)
        for grad, start, ref in ((gk, k_start, gk_ref), (gv, v_start, gv_ref)):
            ref[:near, :] = grad[:near] + start[...]
            ref[near:, :] = grad[near:]
        return
    for start, ref in ((k_start, gk_ref), (v_start, gv_ref)):
        ref[:near, :] = start[...]
        ref[near:, :] = jnp.zeros((plan.seg_rows - near, plan.chunk_width), F32)

    def body(i, _):
        start = pl.multiple_of(i * near, near)
        gq, gk, gv = group(start)
        gq_ref[pl.ds(start, near), :] = gq.astype(BF16)
        gk_ref[pl.ds(start, 2 * near), :] += gk
        gv_ref[pl.ds(start, 2 * near), :] += gv
        return 0

    lax.fori_loop(0, plan.groups - 1, body, 0)


def rest_groups(plan, held, starts):
    near, width = plan.near, plan.chunk_width
    count = plan.seg_rows - near
    outs = [
        shape((count, width)),
        shape((plan.seg_rows, width), F32),
        shape((plan.seg_rows, width), F32),
    ]
    flops = 24 * plan.heads * count * near * plan.dim
    return call(functools.partial(rest_kernel, plan), list(held) + list(starts), outs, (), flops)


def finish_kernel(plan, gq_first, gq_rest, gk, gv, far, *refs):
    me = lax.axis_index("dev")
    out_refs, (grads,) = refs[: plan.devs], refs[plan.devs :]
    near = plan.near
    last = plan.seg_rows - near
    grads[0, :near, :] = gq_first[...]
    grads[0, near:, :] = gq_rest[...]
    for at, ref in enumerate((gk, gv)):
        grads[1 + at, :last, :] = ref[:last, :].astype(BF16)
        for block in range(plan.reach):
            groups = unfolded(far[block, at], plan)
            for part, rows in block_parts(last + block * plan.rows, plan):
                grads[1 + at, rows, :] = (ref[rows, :] + groups[part].astype(F32)).astype(BF16)
    for step, out_ref in enumerate(out_refs):
        rows = pl.ds(pl.multiple_of((me ^ step) * plan.rows, plan.rows), plan.rows)
        for at in range(3):
            out_ref[at] = folded(grads[at, rows, :], plan)


def finish(plan, gq_first, gq_rest, gk, gv, far):
    outs = [shape((3,) + plan.piece) for _ in range(plan.devs)]
    scratch = [pltpu.VMEM((3, plan.seg_rows, plan.chunk_width), BF16)]
    arrays = [gq_first, gq_rest, gk, gv, far]
    return call(functools.partial(finish_kernel, plan), arrays, outs, scratch)


def local(queries, keys, values):
    rows, width = queries.shape
    plan = Plan(rows, width, lax.axis_size("dev"))
    seg_count = lax.axis_size("seg")
    onward = [(i, i + 1) for i in range(seg_count - 1)]
    backward = [(i + 1, i) for i in range(seg_count - 1)]
    me = lax.axis_index("dev")
    packed = pack(plan, [queries, keys, values])
    arrived = []
    for pieces in packed:
        arrived.append(exchange(plan, pieces))
    returned = []
    for pieces in arrived:
        halo = jnp.stack(
            [
                lax.select_n((plan.devs - plan.reach + b) ^ me, *[p[1:] for p in pieces])
                for b in range(plan.reach)
            ]
        )
        halo = lax.ppermute(halo, "seg", onward)
        held = teacher(plan, pieces)
        gq_first, gk, gv, far = first_group(plan, held, halo)
        far = lax.ppermute(far, "seg", backward)
        gq_rest, gk, gv = rest_groups(plan, held, (gk, gv))
        pieces = finish(plan, gq_first, gq_rest, gk, gv, far)
        returned.append(exchange(plan, pieces))
    return tuple(unpack(plan, returned))


def solution(mesh):
    spec = P(("seg", "dev"), None)
    return jax.shard_map(
        local, mesh=mesh, in_specs=(spec,) * 3, out_specs=(spec,) * 3, check_vma=False
    )
```

```python
import functools
import math

import jax
import jax.numpy as jnp
from jax import lax
from jax.experimental import pallas as pl
from jax.experimental.pallas import tpu as pltpu
from jax.sharding import PartitionSpec as P


HEADS = 16
WINDOW = 256
CHUNKS = 2
NEGATIVE = -1e30
LOG2E = math.log2(math.e)
BF16 = jnp.bfloat16
F32 = jnp.float32


VMEM_SPEC = pl.BlockSpec(memory_space=pltpu.VMEM)
HBM_SPEC = pl.BlockSpec(memory_space=pltpu.HBM)


def call(kernel, arrays, outs, scratch=(), flops=0, spec=VMEM_SPEC, out_spec=VMEM_SPEC):
    moved = sum(a.size * a.dtype.itemsize for a in arrays)
    moved += sum(math.prod(o.shape) * o.dtype.itemsize for o in outs)
    return pl.pallas_call(
        kernel,
        out_shape=tuple(outs),
        in_specs=[spec] * len(arrays),
        out_specs=tuple([out_spec] * len(outs)),
        scratch_shapes=list(scratch),
        cost_estimate=pl.CostEstimate(flops=flops, bytes_accessed=moved, transcendentals=0),
        compiler_params=pltpu.CompilerParams(vmem_limit_bytes=48 * 1024 * 1024),
    )(*arrays)


def shape(dims, dtype=BF16):
    return jax.ShapeDtypeStruct(dims, dtype)


class Plan:
    def __init__(self, rows, width, devs):
        self.rows, self.width, self.devs = rows, width, devs
        self.dim = width // HEADS
        self.local_heads = HEADS // devs
        self.local_width = width // devs
        self.chunks = CHUNKS if self.local_heads % CHUNKS == 0 else 1
        self.heads = self.local_heads // self.chunks
        self.chunk_width = self.heads * self.dim
        self.fold = 128 // math.gcd(self.chunk_width, 128)
        self.fold_rows = rows // self.fold
        self.piece = (self.fold_rows, self.fold * self.chunk_width)
        self.reach = WINDOW // rows
        self.seg_rows = rows * devs
        self.near = self.reach * rows
        self.groups = self.seg_rows // self.near
        self.scale = self.dim ** (-0.5)


def folded(x, plan):
    full = plan.chunk_width // 128 * 128
    parts = [x[i * plan.fold_rows : (i + 1) * plan.fold_rows] for i in range(plan.fold)]
    columns = [p[:, at : at + 128] for at in range(0, full, 128) for p in parts]
    if plan.chunk_width > full:
        columns += [p[:, full:] for p in parts]
    return columns[0] if len(columns) == 1 else jnp.concatenate(columns, axis=1)


def unfolded(x, plan):
    full = plan.chunk_width // 128 * 128
    rest = plan.chunk_width - full
    groups = []
    for i in range(plan.fold):
        columns = [
            x[:, at * plan.fold + i * 128 : at * plan.fold + (i + 1) * 128]
            for at in range(0, full, 128)
        ]
        if rest:
            start = plan.fold * full + i * rest
            columns.append(x[:, start : start + rest])
        groups.append(columns[0] if len(columns) == 1 else jnp.concatenate(columns, axis=1))
    return groups


def columns_of(x, chunk, plan):
    return folded(x[:, chunk * plan.chunk_width : (chunk + 1) * plan.chunk_width], plan)


def pack_first_kernel(plan, steps, *refs):
    me = lax.axis_index("dev")
    in_refs, out_refs, (held, sems) = refs[:3], refs[3:-2], refs[-2:]

    def taken(i, at):
        start = pl.multiple_of((me ^ steps[i]) * plan.local_width, 128)
        block = in_refs[at].at[:, pl.ds(start, plan.local_width)]
        return pltpu.make_async_copy(block, held.at[i, at], sems.at[i, at])

    each = [(i, at) for i in range(len(steps)) for at in range(3)]
    for i, at in each:
        taken(i, at).start()
    for i, at in each:
        taken(i, at).wait()
        out_refs[i][at] = columns_of(held[i, at], 0, plan)


def pack_rest_kernel(plan, chunk, *refs):
    me = lax.axis_index("dev")
    in_refs, out_refs = refs[:3], refs[3:]
    for at in range(3):
        for step in range(plan.devs):
            start = pl.multiple_of((me ^ step) * plan.local_width, 128)
            x = in_refs[at][:, pl.ds(start, plan.local_width)]
            out_refs[step][at] = columns_of(x, chunk, plan)
            if chunk == 1 and step == 0:
                out_refs[plan.devs][at] = columns_of(x, 0, plan)


def pack(plan, arrays):
    piece = shape((3,) + plan.piece)
    chunks = []
    if plan.local_width % 128 == 0 and plan.chunks > 1:
        sent = [None] * plan.devs
        far_away = plan.devs - 1
        held = [pltpu.with_memory_space_constraint(a, pltpu.HBM) for a in arrays]
        for steps in [[step] for step in range(far_away, 0, -1)]:
            scratch = [
                pltpu.VMEM((len(steps), 3, plan.rows, plan.local_width), BF16),
                pltpu.SemaphoreType.DMA((len(steps), 3)),
            ]
            kernel = functools.partial(pack_first_kernel, plan, steps)
            got = call(kernel, held, [piece] * len(steps), scratch, spec=HBM_SPEC)
            for step, x in zip(steps, got):
                sent[step] = x
        chunks.append(sent)
        for chunk in range(1, plan.chunks):
            kernel = functools.partial(pack_rest_kernel, plan, chunk)
            got = list(call(kernel, arrays, [piece] * (plan.devs + (chunk == 1))))
            if chunk == 1:
                chunks[0][0] = got.pop()
            chunks.append(got)
        return chunks
    me = lax.axis_index("dev")
    for chunk in range(plan.chunks):
        pieces = []
        for step in range(plan.devs):
            start = (me ^ step) * plan.local_width + chunk * plan.chunk_width
            taken = [lax.dynamic_slice_in_dim(a, start, plan.chunk_width, 1) for a in arrays]
            pieces.append(jnp.stack([folded(x, plan) for x in taken]))
        chunks.append(pieces)
    return chunks


def unpack_kernel(plan, *refs):
    me = lax.axis_index("dev")
    piece_refs, out_refs, (held, sems) = refs[:-5], refs[-5:-2], refs[-2:]

    def given(step, at):
        start = pl.multiple_of((me ^ step) * plan.local_width, 128)
        block = out_refs[at].at[:, pl.ds(start, plan.local_width)]
        return pltpu.make_async_copy(held.at[step, at], block, sems.at[step, at])

    for step in range(plan.devs):
        for at in range(3):
            got = [unfolded(piece_refs[c * plan.devs + step][at], plan) for c in range(plan.chunks)]
            for part in range(plan.fold):
                rows = slice(part * plan.fold_rows, (part + 1) * plan.fold_rows)
                x = [groups[part] for groups in got]
                held[step, at, rows, :] = x[0] if plan.chunks == 1 else jnp.concatenate(x, axis=1)
            given(step, at).start()
    for step in range(plan.devs):
        for at in range(3):
            given(step, at).wait()


def unpack(plan, pieces):
    if plan.local_width % 128 == 0:
        flat = [piece for chunk in pieces for piece in chunk]
        outs = [shape((plan.rows, plan.width)) for _ in range(3)]
        scratch = [
            pltpu.VMEM((plan.devs, 3, plan.rows, plan.local_width), BF16),
            pltpu.SemaphoreType.DMA((plan.devs, 3)),
        ]
        kernel = functools.partial(unpack_kernel, plan)
        return call(kernel, flat, outs, scratch, out_spec=HBM_SPEC)
    order = jnp.arange(plan.devs, dtype=jnp.int32) ^ lax.axis_index("dev")
    chunks = []
    for chunk in pieces:
        x = jnp.take(jnp.stack(chunk), order, axis=0)
        x = [jnp.concatenate(unfolded(x[d, at], plan), 0) for d in range(plan.devs) for at in range(3)]
        x = jnp.stack(x).reshape(plan.devs, 3, plan.rows, plan.chunk_width)
        chunks.append(x.transpose(1, 2, 0, 3))
    out = jnp.concatenate(chunks, axis=3).reshape(3, plan.rows, plan.width)
    return out[0], out[1], out[2]


def exchange(plan, pieces):
    got = [pieces[0]] + [None] * (plan.devs - 1)
    for step in range(plan.devs - 1, 0, -1):
        pairs = [(i, i ^ step) for i in range(plan.devs)]
        got[step] = lax.ppermute(pieces[step], "dev", pairs)
    return got


def dot(a, b, over):
    return lax.dot_general(a, b, ((over[:1], over[1:]), ((), ())), preferred_element_type=F32)


def dot_heads(parts, b, over):
    axis = 1 - over[0]
    count = parts[0].shape[axis]
    out = dot(jnp.concatenate(parts, axis=axis), b, over)
    return [out[i * count : (i + 1) * count] for i in range(len(parts))]


def of_head(x, head, plan):
    if plan.heads == 1:
        return x
    lane = lax.broadcasted_iota(jnp.int32, x.shape, 1)
    own = (lane >= head * plan.dim) & (lane < (head + 1) * plan.dim)
    return jnp.where(own, x, jnp.zeros_like(x))


def joined(parts, plan):
    columns = []
    for first in range(0, plan.chunk_width, 128):
        end = min(first + 128, plan.chunk_width)
        out = None
        for head in range(plan.heads):
            if head * plan.dim >= end or (head + 1) * plan.dim <= first:
                continue
            x = parts[head][:, first:end]
            if out is None:
                out = x
            else:
                lane = first + lax.broadcasted_iota(jnp.int32, x.shape, 1)
                out = jnp.where(lane < head * plan.dim, out, x)
        columns.append(out)
    return columns[0] if len(columns) == 1 else jnp.concatenate(columns, axis=1)


def block_parts(first, plan):
    for part in range(plan.fold):
        start = first + part * plan.fold_rows
        yield part, pl.ds(pl.multiple_of(start, plan.fold_rows), plan.fold_rows)


def teacher_rows(plan, q, k, v):
    parts = []
    scores = [dot(of_head(q, head, plan), k, (1, 1)) for head in range(plan.heads)]
    for s in scores:
        e = jnp.exp2((s - s.max(-1, keepdims=True)) * (plan.scale * LOG2E))
        parts.append(dot(e.astype(BF16), v, (1, 0)) * (1.0 / e.sum(-1, keepdims=True)))
    return joined(parts, plan).astype(BF16)


def student_group(plan, q, k, v, target, open_far):
    rows, reach, heads = plan.rows, plan.reach, range(plan.heads)
    at_query = lax.broadcasted_iota(jnp.int32, (rows, rows), 0)
    at_key = lax.broadcasted_iota(jnp.int32, (rows, rows), 1)
    late, early = at_key >= at_query, at_key <= at_query

    def seen(i, block, j):
        mask = None
        if j == i:
            mask = late
        elif j == i + reach:
            mask = early
        if open_far is not None and j < reach:
            mask = jnp.broadcast_to(open_far, (rows, rows)) if mask is None else mask & open_far
        return block if mask is None else jnp.where(mask, block, NEGATIVE)

    def window(x, i):
        return x[i * rows : (i + 1) * rows, i * rows : (i + reach + 1) * rows]

    def whole(parts):
        lines = []
        for i, x in enumerate(parts):
            left = [jnp.zeros((rows, i * rows), x.dtype)] if i else []
            right = [jnp.zeros((rows, (reach - 1 - i) * rows), x.dtype)] if i < reach - 1 else []
            lines.append(jnp.concatenate(left + [x] + right, axis=1))
        return lines[0] if reach == 1 else jnp.concatenate(lines, axis=0)

    scores = [dot(of_head(q, head, plan), k, (1, 1)) for head in heads]
    weights, probability, outs = [], [], []
    for head in heads:
        ps = []
        for i in range(reach):
            s = window(scores[head], i)
            s = [seen(i, s[:, j * rows : (j + 1) * rows], i + j) for j in range(reach + 1)]
            s = jnp.concatenate(s, axis=1)
            top = s.max(-1, keepdims=True)
            e = jnp.exp2((s - top) * (plan.scale * LOG2E))
            ps.append(e * (1.0 / e.sum(-1, keepdims=True)))
        probability.append(ps)
        weights.append(whole([p.astype(BF16) for p in ps]))
        outs.append(dot(weights[head], v, (1, 0)))
    d_out = (128.0 * (joined(outs, plan) - target.astype(F32))).astype(BF16)
    d_prob = [dot(of_head(d_out, head, plan), v, (1, 1)) for head in heads]
    gv = dot_heads(weights, d_out, (0, 0))
    d_scores = []
    for head in heads:
        ds = []
        for i, p in enumerate(probability[head]):
            d = window(d_prob[head], i)
            inner = (p * d).sum(-1, keepdims=True)
            ds.append((p * (d - inner) * plan.scale).astype(BF16))
        d_scores.append(whole(ds))
    gk = dot_heads(d_scores, q, (0, 0))
    gq = dot_heads(d_scores, k, (1, 0))
    return joined(gq, plan), joined(gk, plan), joined(gv, plan)


def teacher_kernel(plan, *refs):
    me = lax.axis_index("dev")
    piece_refs, (q_ref, k_ref, v_ref, target_ref) = refs[: plan.devs], refs[plan.devs :]
    for step, ref in enumerate(piece_refs):
        for at, to in enumerate((q_ref, k_ref, v_ref)):
            groups = unfolded(ref[at], plan)
            for part, rows in block_parts((me ^ step) * plan.rows, plan):
                to[rows, :] = groups[part]
    target_ref[...] = teacher_rows(plan, q_ref[: plan.near, :], k_ref[...], v_ref[...])


def teacher(plan, pieces):
    outs = [shape((plan.seg_rows, plan.chunk_width))] * 3 + [shape((plan.near, plan.chunk_width))]
    flops = 4 * plan.heads * plan.near * plan.seg_rows * plan.dim
    return call(functools.partial(teacher_kernel, plan), list(pieces), outs, (), flops)


def first_kernel(plan, q_ref, k_ref, v_ref, target_ref, halo_ref, gq_ref, gk_ref, gv_ref, far_ref, ext):
    near = plan.near
    for at, ref in enumerate((k_ref, v_ref)):
        for block in range(plan.reach):
            groups = unfolded(halo_ref[block, at], plan)
            for part, rows in block_parts(block * plan.rows, plan):
                ext[at, rows, :] = groups[part]
        ext[at, near:, :] = ref[:near, :]
    open_far = lax.axis_index("seg") > 0
    gq, gk, gv = student_group(plan, q_ref[:near, :], ext[0], ext[1], target_ref[...], open_far)
    gq_ref[...] = gq.astype(BF16)
    for at, (grad, ref) in enumerate(((gk, gk_ref), (gv, gv_ref))):
        ref[...] = grad[near:]
        for block in range(plan.reach):
            rows = slice(block * plan.rows, (block + 1) * plan.rows)
            far_ref[block, at] = folded(grad[rows].astype(BF16), plan)


def first_group(plan, held, halo):
    near, width = plan.near, plan.chunk_width
    outs = [
        shape((near, width)),
        shape((near, width), F32),
        shape((near, width), F32),
        shape((plan.reach, 2) + plan.piece),
    ]
    scratch = [pltpu.VMEM((2, 2 * near, width), BF16)]
    flops = 24 * plan.heads * near * near * plan.dim
    return call(functools.partial(first_kernel, plan), list(held) + [halo], outs, scratch, flops)


def rest_kernel(plan, q_ref, k_ref, v_ref, k_start, v_start, gq_ref, gk_ref, gv_ref):
    near = plan.near

    def group(start):
        rows, keys = pl.ds(start + near, near), pl.ds(start, 2 * near)
        target = teacher_rows(plan, q_ref[rows, :], k_ref[...], v_ref[...])
        return student_group(plan, q_ref[rows, :], k_ref[keys, :], v_ref[keys, :], target, None)

    if plan.groups == 2:
        gq, gk, gv = group(0)
        gq_ref[...] = gq.astype(BF16)
        for grad, start, ref in ((gk, k_start, gk_ref), (gv, v_start, gv_ref)):
            ref[:near, :] = grad[:near] + start[...]
            ref[near:, :] = grad[near:]
        return
    for start, ref in ((k_start, gk_ref), (v_start, gv_ref)):
        ref[:near, :] = start[...]
        ref[near:, :] = jnp.zeros((plan.seg_rows - near, plan.chunk_width), F32)

    def body(i, _):
        start = pl.multiple_of(i * near, near)
        gq, gk, gv = group(start)
        gq_ref[pl.ds(start, near), :] = gq.astype(BF16)
        gk_ref[pl.ds(start, 2 * near), :] += gk
        gv_ref[pl.ds(start, 2 * near), :] += gv
        return 0

    lax.fori_loop(0, plan.groups - 1, body, 0)


def rest_groups(plan, held, starts):
    near, width = plan.near, plan.chunk_width
    count = plan.seg_rows - near
    outs = [
        shape((count, width)),
        shape((plan.seg_rows, width), F32),
        shape((plan.seg_rows, width), F32),
    ]
    flops = plan.heads * count * plan.dim * (24 * near + 4 * plan.seg_rows)
    return call(functools.partial(rest_kernel, plan), list(held) + list(starts), outs, (), flops)


def finish_kernel(plan, gq_first, gq_rest, gk, gv, far, *refs):
    me = lax.axis_index("dev")
    out_refs, (grads,) = refs[: plan.devs], refs[plan.devs :]
    near = plan.near
    last = plan.seg_rows - near
    grads[0, :near, :] = gq_first[...]
    grads[0, near:, :] = gq_rest[...]
    for at, ref in enumerate((gk, gv)):
        grads[1 + at, :last, :] = ref[:last, :].astype(BF16)
        for block in range(plan.reach):
            groups = unfolded(far[block, at], plan)
            for part, rows in block_parts(last + block * plan.rows, plan):
                grads[1 + at, rows, :] = (ref[rows, :] + groups[part].astype(F32)).astype(BF16)
    for step, out_ref in enumerate(out_refs):
        rows = pl.ds(pl.multiple_of((me ^ step) * plan.rows, plan.rows), plan.rows)
        for at in range(3):
            out_ref[at] = folded(grads[at, rows, :], plan)


def finish(plan, gq_first, gq_rest, gk, gv, far):
    outs = [shape((3,) + plan.piece) for _ in range(plan.devs)]
    scratch = [pltpu.VMEM((3, plan.seg_rows, plan.chunk_width), BF16)]
    arrays = [gq_first, gq_rest, gk, gv, far]
    return call(functools.partial(finish_kernel, plan), arrays, outs, scratch)


def local(queries, keys, values):
    rows, width = queries.shape
    plan = Plan(rows, width, lax.axis_size("dev"))
    seg_count = lax.axis_size("seg")
    onward = [(i, i + 1) for i in range(seg_count - 1)]
    backward = [(i + 1, i) for i in range(seg_count - 1)]
    me = lax.axis_index("dev")
    packed = pack(plan, [queries, keys, values])
    arrived = []
    for pieces in packed:
        arrived.append(exchange(plan, pieces))
    returned = []
    for pieces in arrived:
        halo = jnp.stack(
            [
                lax.select_n((plan.devs - plan.reach + b) ^ me, *[p[1:] for p in pieces])
                for b in range(plan.reach)
            ]
        )
        halo = lax.ppermute(halo, "seg", onward)
        held = teacher(plan, pieces)
        gq_first, gk, gv, far = first_group(plan, held, halo)
        far = lax.ppermute(far, "seg", backward)
        gq_rest, gk, gv = rest_groups(plan, held[:3], (gk, gv))
        pieces = finish(plan, gq_first, gq_rest, gk, gv, far)
        returned.append(exchange(plan, pieces))
    return tuple(unpack(plan, returned))


def solution(mesh):
    spec = P(("seg", "dev"), None)
    return jax.shard_map(
        local, mesh=mesh, in_specs=(spec,) * 3, out_specs=(spec,) * 3, check_vma=False
    )
```
